256 devices in a mesh: row: 16 (over x_lo, y, core), col: 16 (over z, x_hi).
Axes of the slice: x: 4 (x_hi: 2, x_lo: 2; x = x_hi * 2 + x_lo), y: 4, z: 8, core: 2. Of those that a mesh axis runs over, the one named last changes fastest.
Arguments:
- images: bfloat16 [2, 64, 64, 2048], P(None, 'row', None, 'col'), may hold values from -6 to 6
- dw_kernel: float32 [7, 7, 2048], P(None, None, 'col'), may hold values from -3 to 3
- norm_gain: float32 [2048], P('col'), may hold values from 0.5 to 1.5
- proj_in: bfloat16 [2048, 8192], P('row', 'col'), may hold values from -0.125 to 0.125
- proj_out: bfloat16 [2048, 8192], P('row', 'col'), may hold values from -0.0625 to 0.0625
- layer_scale: float32 [2048], P('col'), may hold values from 0.1 to 1.9
- cotangent: bfloat16 [2, 64, 64, 2048], P(None, 'row', None, 'col'), may hold values from -0.59765625 to 0.59765625
Outputs:
- block_out: bfloat16 [2, 64, 64, 2048], P(None, 'row', None, 'col')
- grad_images: bfloat16 [2, 64, 64, 2048], P(None, 'row', None, 'col')
- grad_proj_in: bfloat16 [2048, 8192], P('row', 'col')
- grad_proj_out: bfloat16 [2048, 8192], P('row', 'col')
The draws below stay inside these ranges and needn't reach their ends.
All inputs are finite; a program needn't handle non-finite values.
Results may differ from the reference program's by a relative error of at most 0.023.
Values may be sent and summed in bfloat16 or wider, within the bound.
A program may use at most 64 MiB of HBM per device.

```python
import jax
import jax.numpy as jnp
from jax import lax

C = 2048
HID = 8192
KS = 7
STRIP = 4
IMG_W = 64
BATCH = 2
IMG_H = 64
N_ROW = 16
N_COL = 16


def draw_dw_kernel(key, part):
    first_key, second_key = jax.random.split(key)
    channel = jnp.arange(C, dtype=jnp.float32) / max(C - 1, 1)
    jitter = jnp.exp(jax.random.uniform(second_key, (C,), jnp.float32, jnp.log(0.7), jnp.log(1.4)))
    factor = jnp.exp(jnp.log(3.0) * channel) * jitter
    taps = jax.random.truncated_normal(first_key, -3.0, 3.0, (KS, KS, C), jnp.float32) / 7.0
    return (taps * factor).astype(jnp.float32)


def raised(array, own_key, source, target, shards_of, factor):
    owner, partner = [(jnp.arange(array.shape[position]) // (array.shape[position] // shards_of)).reshape([-1 if axis == position else 1 for axis in range(array.ndim)]) for position in (source, target)]
    chosen = jax.random.permutation(own_key, shards_of)[partner]
    strong = (owner == chosen) | (owner == (partner + shards_of // 2) % shards_of)
    return jnp.where(strong, factor * array, array)


def block_levels(rng, shape, cuts, smallest, largest):
    gain = 1.0
    for dim, blocks in cuts:
        steps = jax.random.uniform(jax.random.fold_in(jax.random.fold_in(rng, 6), dim), (blocks,), jnp.float32, smallest / len(cuts), largest / len(cuts))
        gain = gain * jnp.repeat(jnp.exp(steps), shape[dim] // blocks).reshape((-1,) + (1,) * (len(shape) - 1 - dim))
    return gain


def scatter_about(stream_key, extent, scale, most, cuts=(), held_as=jnp.bfloat16):
    result = scale * jax.random.normal(stream_key, extent, jnp.float32)
    if cuts:
        result = result * block_levels(stream_key, extent, cuts, -0.22, 0.18)
    return jnp.clip(result, -most, most).astype(held_as)


def bell_draw_with(own_key, dims, deviation, most, cuts, heavy, held_as=jnp.bfloat16):
    values = deviation * jax.random.normal(own_key, dims, jnp.float32)
    if cuts:
        values = values * block_levels(own_key, dims, cuts, -0.22, 0.18)
    return jnp.clip(raised(values, jax.random.fold_in(own_key, 3), *heavy), -most, most).astype(held_as)


def setup_inputs(seed: int = 0) -> dict:
    key_of = jax.random.split(jax.random.key(seed), 8)
    return {
        "images": scatter_about(key_of[0], (BATCH, IMG_H, IMG_W, C), 1.0, 6.0, ((1, 16), (3, 16))),
        "dw_kernel": draw_dw_kernel(jax.random.fold_in(key_of[7], 71), 0),
        "norm_gain": jnp.clip(1.0 + 0.1 * jax.random.normal(key_of[2], (C,), jnp.float32), 0.5, 1.5),
        "proj_in": scatter_about(key_of[3], (C, HID), C ** -0.5, 0.125, ((0, 16), (1, 16))),
        "proj_out": scatter_about(key_of[4], (C, HID), HID ** -0.5, 0.0625, ((0, 16), (1, 16))),
        "layer_scale": jnp.clip(1.0 + 0.18 * jax.random.normal(key_of[5], (C,), jnp.float32), 0.1, 1.9),
        "cotangent": bell_draw_with(key_of[6], (BATCH, IMG_H, IMG_W, C), 0.1, 0.59765625, ((1, 16), (3, 16)), (1, 3, 16, 2.0)),
    }


def rounded(partial_sum):
    return lax.optimization_barrier(partial_sum.astype(jnp.bfloat16)).astype(jnp.float32)

def taps_sum(padded, dw_kernel, img_rows, img_cols, flipped):
    total = jnp.zeros(padded.shape[:1] + (img_rows, img_cols) + padded.shape[3:], jnp.float32)
    reach = 2 * (KS // 2)
    for tap_row in range(KS):
        for tap_col in range(KS):
            off_row = reach - tap_row if flipped else tap_row
            off_col = reach - tap_col if flipped else tap_col
            total = total + dw_kernel[tap_row, tap_col] * padded[:, off_row:off_row + img_rows, off_col:off_col + img_cols, :]
    return total

def gelu_slope(values):
    return 0.5 * (1.0 + lax.erf(values * 0.7071067811865476)) + values * jnp.exp(-0.5 * values * values) * 0.3989422804014327

def reference(images, dw_kernel, norm_gain, proj_in, proj_out, layer_scale, cotangent):
    pixels = BATCH * IMG_H * IMG_W
    reach = KS // 2
    padded = jnp.pad(images.astype(jnp.float32), ((0, 0), (reach, reach), (reach, reach), (0, 0)))
    conv_out = taps_sum(padded, dw_kernel, IMG_H, IMG_W, False).reshape(pixels, C)
    row_mean = lax.optimization_barrier(jnp.mean(conv_out, axis=1))
    centred = conv_out - row_mean[:, None]
    row_var = lax.optimization_barrier(jnp.mean(centred * centred, axis=1))
    inv_std = lax.rsqrt(row_var + 1e-06)
    normed = centred * inv_std[:, None]
    scaled = (normed * norm_gain).astype(jnp.bfloat16)
    hidden_pre = jnp.dot(scaled, proj_in, preferred_element_type=jnp.float32)
    hidden = jax.nn.gelu(hidden_pre, approximate=False).astype(jnp.bfloat16)
    hid_cols = HID // N_COL
    contract_last = (((1,), (1,)), ((), ()))
    contract_first = (((0,), (0,)), ((), ()))

    def add_branch(index, total):
        first_col = jnp.asarray(index, jnp.int32) * hid_cols
        act_block = lax.dynamic_slice_in_dim(hidden, first_col, hid_cols, 1)
        weight_block = lax.dynamic_slice_in_dim(proj_out, first_col, hid_cols, 1)
        return total + rounded(lax.dot_general(act_block, weight_block, contract_last, preferred_element_type=jnp.float32))
    branch = lax.fori_loop(0, N_COL, add_branch, jnp.zeros((pixels, C), jnp.float32))
    block_out = (images.reshape(pixels, C).astype(jnp.float32) + layer_scale * branch).astype(jnp.bfloat16)
    cot_flat = cotangent.reshape(pixels, C).astype(jnp.float32)
    grad_branch = (cot_flat * layer_scale).astype(jnp.bfloat16)
    grad_hidden = jnp.dot(grad_branch, proj_out, preferred_element_type=jnp.float32)
    grad_pre = (grad_hidden * gelu_slope(hidden_pre)).astype(jnp.bfloat16)
    strip_pix = STRIP * IMG_W
    branch_strips = grad_branch.reshape(BATCH, N_ROW, strip_pix, C)
    hidden_strips = hidden.reshape(BATCH, N_ROW, strip_pix, HID)
    scaled_strips = scaled.reshape(BATCH, N_ROW, strip_pix, C)
    pre_strips = grad_pre.reshape(BATCH, N_ROW, strip_pix, HID)

    def add_grads(index, totals):
        idx = jnp.asarray(index, jnp.int32)
        grad_rows = lax.dynamic_index_in_dim(branch_strips, idx, 1, keepdims=False).reshape(-1, C)
        act_rows = lax.dynamic_index_in_dim(hidden_strips, idx, 1, keepdims=False).reshape(-1, HID)
        norm_rows = lax.dynamic_index_in_dim(scaled_strips, idx, 1, keepdims=False).reshape(-1, C)
        pre_rows = lax.dynamic_index_in_dim(pre_strips, idx, 1, keepdims=False).reshape(-1, HID)
        out_term = lax.dot_general(grad_rows, act_rows, contract_first, preferred_element_type=jnp.float32)
        in_term = lax.dot_general(norm_rows, pre_rows, contract_first, preferred_element_type=jnp.float32)
        return (totals[0] + rounded(out_term), totals[1] + rounded(in_term))
    zero_grads = (jnp.zeros((C, HID), jnp.float32), jnp.zeros((C, HID), jnp.float32))
    out_total, in_total = lax.fori_loop(0, N_ROW, add_grads, zero_grads)
    grad_proj_out = out_total.astype(jnp.bfloat16)
    grad_proj_in = in_total.astype(jnp.bfloat16)

    def add_input(index, total):
        first_col = jnp.asarray(index, jnp.int32) * hid_cols
        pre_block = lax.dynamic_slice_in_dim(grad_pre, first_col, hid_cols, 1)
        weight_block = lax.dynamic_slice_in_dim(proj_in, first_col, hid_cols, 1)
        return total + rounded(lax.dot_general(pre_block, weight_block, contract_last, preferred_element_type=jnp.float32))
    grad_scaled = lax.fori_loop(0, N_COL, add_input, jnp.zeros((pixels, C), jnp.float32))
    weighted = grad_scaled * norm_gain
    mean_one = lax.optimization_barrier(jnp.mean(weighted, axis=1))
    mean_two = lax.optimization_barrier(jnp.mean(weighted * normed, axis=1))
    grad_conv = inv_std[:, None] * (weighted - mean_one[:, None] - normed * mean_two[:, None])
    grad_conv = grad_conv.reshape(BATCH, IMG_H, IMG_W, C)
    grad_pad = jnp.pad(grad_conv, ((0, 0), (reach, reach), (reach, reach), (0, 0)))
    input_grad = taps_sum(grad_pad, dw_kernel, IMG_H, IMG_W, True)
    grad_images = (cotangent.astype(jnp.float32) + input_grad).astype(jnp.bfloat16)
    return (block_out.reshape(BATCH, IMG_H, IMG_W, C), grad_images, grad_proj_in, grad_proj_out)
```

```python
import functools

import jax
import jax.numpy as jnp
from jax import lax
from jax.experimental import pallas as pl
from jax.experimental.pallas import tpu as pltpu
from jax.sharding import PartitionSpec as P

MESH = pl.DeviceIdType.MESH
F32, BF16 = jnp.float32, jnp.bfloat16
C = 2048
KS = 7
NZ, NY = 8, 4
CB = 128
HB = 512
PIX = 512
LEFT = 8
TAP0 = LEFT - KS // 2
N_SEMS = 256
CONTRACT_LAST = (((1,), (1,)), ((), ()))
CONTRACT_FIRST = (((0,), (0,)), ((), ()))


def kernel(
    n0,
    images, dwk, gain, w_in, w_out, lscale, cot,
    block_out, grad_images, gp_in, gp_out,
    pad, halo_lo, halo_hi, ghalo_lo, ghalo_hi, edge_lo, edge_hi,
    conv, normed, istd, tmp, st1, st2,
    xg, gg, wi, wo, hp, gh, hid, gpre,
    cb, bk, cb_m, cb_p, bk_m, bk_p, cb_m1, cb_p1, bk_m1, bk_p1,
    cb_x, bk_x, cb_xs, bk_xs, cb_xr, bk_xr, gs,
    g1, g2, g1_c, g2_c, g1_m, g1_p, g2_m, g2_p, g1_r, g2_r,
    send_sem, recv_sem,
):
    n1 = PIX - n0
    row, col = lax.axis_index("row"), lax.axis_index("col")
    xlo, y, core = row // 8, (row // 2) % NY, row % 2
    z, xhi = col // 2, col % 2

    def at_z(step):
        return (z + step + NZ) % NZ

    def at_y(step):
        return (y + step + NY) % NY

    z_up = {"row": row, "col": at_z(1) * 2 + xhi}
    z_down = {"row": row, "col": at_z(-1) * 2 + xhi}
    x_far = {"row": row, "col": z * 2 + (1 - xhi)}
    y_up = {"row": xlo * 8 + at_y(1) * 2 + core, "col": col}
    y_down = {"row": xlo * 8 + at_y(-1) * 2 + core, "col": col}
    x_near = {"row": (1 - xlo) * 8 + y * 2 + core, "col": col}
    sibling = {"row": xlo * 8 + y * 2 + (1 - core), "col": col}
    strip_up = {"row": (row + 1) % 16, "col": col}
    strip_down = {"row": (row + 15) % 16, "col": col}

    def col_peer(step):
        return {"row": row, "col": (col + step) % 16}

    started = []

    def send(src, dst, where):
        index = len(started)
        copy = pltpu.make_async_remote_copy(
            src_ref=src, dst_ref=dst, send_sem=send_sem.at[index], recv_sem=recv_sem.at[index],
            device_id=where, device_id_type=MESH,
        )
        copy.start()
        started.append(copy)
        return copy

    barrier = pltpu.get_barrier_semaphore()
    peers = [strip_up, strip_down, y_up, y_down, x_near] + [col_peer(k) for k in range(1, 16)]
    for peer in peers:
        pl.semaphore_signal(barrier, inc=1, device_id=peer, device_id_type=MESH)
    pl.semaphore_wait(barrier, len(peers))

    def ring_gather(buf, half, first, count):
        def block(zi, lo=0, n=count):
            return buf.at[zi, half, pl.ds(first + lo, n)]
        up = send(block(z), block(z), z_up)
        down = send(block(z), block(z), z_down)
        yield
        for k in (1, 2, 3):
            up.wait_recv()
            down.wait_recv()
            if k < 3:
                up = send(block(at_z(-k)), block(at_z(-k)), z_up)
                down = send(block(at_z(k)), block(at_z(k)), z_down)
            else:
                h = count // 2
                up = send(block(at_z(-3), 0, h), block(at_z(-3), 0, h), z_up)
                down = send(block(at_z(3), h, h), block(at_z(3), h, h), z_down)
            yield
        up.wait_recv()
        down.wait_recv()
        yield

    def gather_col(buf):
        def rows(zi, half, first, count):
            return buf.at[zi, half, pl.ds(first, count)]
        waits = {k: [] for k in range(5)}
        rings = []
        if n0:
            far = send(rows(z, xhi, 0, n0), rows(z, xhi, 0, n0), x_far)
            ring = ring_gather(buf, xhi, 0, n0)
            next(ring)
            rings.append(ring)
        if n1:
            ring1 = ring_gather(buf, xhi, n0, n1)
            next(ring1)
            waits[0].append(send(rows(z, xhi, n0, n1), rows(z, xhi, n0, n1), x_far))
        yield
        if n0:
            far.wait_recv()
            ring = ring_gather(buf, 1 - xhi, 0, n0)
            next(ring)
            rings.append(ring)
        yield
        for k in (1, 2, 3, 4):
            if n1:
                next(ring1)
                for step in sorted({-k, k} if k < 4 else {4}):
                    part = rows(at_z(step), xhi, n0, n1)
                    waits[k].append(send(part, part, x_far))
            for ring in rings:
                next(ring)
            if k == 1:
                for copy in waits[0]:
                    copy.wait_recv()
            if k > 1:
                for copy in waits[k - 1]:
                    copy.wait_recv()
            yield
        for copy in waits[4]:
            copy.wait_recv()
        yield

    def gather_row(buf, own):
        def block(k, yi, xi, lo=0, n=CB):
            return buf.at[k, yi, xi, pl.ds(lo, n)]
        waits = []

        def share(yi, xi):
            waits.append(send(block(core, yi, xi), block(core, yi, xi), sibling))

        buf[core, y, xlo] = own[...]
        near = send(own, block(core, y, xlo), x_near)
        up, down = {}, {}
        up[0] = send(own, block(core, y, xlo), y_up)
        down[0] = send(own, block(core, y, xlo), y_down)
        waits.append(send(own, block(core, y, xlo), sibling))
        yield
        near.wait_recv()
        other = 1 - xlo
        up[1] = send(block(core, y, other), block(core, y, other), y_up)
        down[1] = send(block(core, y, other), block(core, y, other), y_down)
        share(y, other)
        yield
        h = CB // 2
        for i, xi in enumerate((xlo, other)):
            up[i].wait_recv()
            down[i].wait_recv()
            low, high = block(core, at_y(-1), xi, 0, h), block(core, at_y(1), xi, h, h)
            up[i] = send(low, low, y_up)
            down[i] = send(high, high, y_down)
            share(at_y(-1), xi)
            share(at_y(1), xi)
            yield
        for i, xi in enumerate((xlo, other)):
            up[i].wait_recv()
            down[i].wait_recv()
            share(at_y(2), xi)
        yield
        for copy in waits:
            copy.wait_recv()
        yield

    def add_into(dst, src):
        dst[...] = (dst[...].astype(F32) + src[...].astype(F32)).astype(BF16)

    def scatter_col(buf, rm, rp, rm1, rp1, rx1, xs, xr, total):
        h0, h1 = n0 // 2, n1 // 2
        if n1:
            first = {}
            for step in (4, -3, 3, -2, 2, -1, 1, 0):
                first[step] = send(
                    buf.at[at_z(step), 1 - xhi, pl.ds(n0, n1)], rx1.at[at_z(step)], x_far
                )
        copies = {}

        def block0(zi, lo=0, n=n0):
            return buf.at[zi, :, pl.ds(lo, n)]

        def block1(zi, lo=0, n=n1):
            return buf.at[zi, xhi, pl.ds(n0 + lo, n)]

        for k in (1, 2, 3, 4):
            dist = 5 - k
            if n0:
                if k == 1:
                    down = send(block0(at_z(-4), 0, h0), rm.at[0, :, pl.ds(0, h0)], z_down)
                    up = send(block0(at_z(4), h0, h0), rp.at[0, :, pl.ds(0, h0)], z_up)
                else:
                    down.wait_recv()
                    if k == 2:
                        add_into(block0(at_z(-dist), 0, h0), rm.at[0, :, pl.ds(0, h0)])
                    else:
                        add_into(block0(at_z(-dist)), rm.at[k - 2])
                    down = send(block0(at_z(-dist)), rm.at[k - 1], z_down)
                    up.wait_recv()
                    if k == 2:
                        add_into(block0(at_z(dist), h0, h0), rp.at[0, :, pl.ds(0, h0)])
                    else:
                        add_into(block0(at_z(dist)), rp.at[k - 2])
                    up = send(block0(at_z(dist)), rp.at[k - 1], z_up)
            if n1:
                if k == 1:
                    first[4].wait_recv()
                    add_into(block1(at_z(4)), rx1.at[at_z(4)])
                    down1 = send(block1(at_z(-4), 0, h1), rm1.at[0, pl.ds(0, h1)], z_down)
                    up1 = send(block1(at_z(4), h1, h1), rp1.at[0, pl.ds(0, h1)], z_up)
                else:
                    first[-dist].wait_recv()
                    add_into(block1(at_z(-dist)), rx1.at[at_z(-dist)])
                    first[dist].wait_recv()
                    add_into(block1(at_z(dist)), rx1.at[at_z(dist)])
                    down1.wait_recv()
                    if k == 2:
                        add_into(block1(at_z(-dist), 0, h1), rm1.at[0, pl.ds(0, h1)])
                    else:
                        add_into(block1(at_z(-dist)), rm1.at[k - 2])
                    down1 = send(block1(at_z(-dist)), rm1.at[k - 1], z_down)
                    up1.wait_recv()
                    if k == 2:
                        add_into(block1(at_z(dist), h1, h1), rp1.at[0, pl.ds(0, h1)])
                    else:
                        add_into(block1(at_z(dist)), rp1.at[k - 2])
                    up1 = send(block1(at_z(dist)), rp1.at[k - 1], z_up)
            yield
        if n0:
            down.wait_recv()
            up.wait_recv()
            theirs = 1 - xhi
            xs[...] = (
                buf[z, theirs, 0:n0].astype(F32)
                + rm[3, theirs].astype(F32)
                + rp[3, theirs].astype(F32)
            ).astype(BF16)
            far = send(xs, xr, x_far)
        if n1:
            first[0].wait_recv()
            down1.wait_recv()
            up1.wait_recv()
            total[n0:PIX] = (
                buf[z, xhi, n0:PIX].astype(F32)
                + rx1[z].astype(F32)
                + rm1[3].astype(F32)
                + rp1[3].astype(F32)
            )
        yield
        if n0:
            far.wait_recv()
            total[0:n0] = (
                buf[z, xhi, 0:n0].astype(F32)
                + rm[3, xhi].astype(F32)
                + rp[3, xhi].astype(F32)
                + xr[...].astype(F32)
            )
        yield

    def scatter_row(buf, rc, rm, rp, rx, xs_slot, out):
        h = CB // 2
        shared = {}
        for step in (2, -1, 1, 0):
            shared[step] = send(buf.at[1 - core, at_y(step)], rc.at[at_y(step)], sibling)
        yield
        shared[2].wait_recv()
        add_into(buf.at[core, at_y(2)], rc.at[at_y(2)])
        down = send(
            buf.at[core, at_y(-2), :, pl.ds(0, h)], rm.at[0, :, pl.ds(0, h)], y_down
        )
        up = send(buf.at[core, at_y(2), :, pl.ds(h, h)], rp.at[0, :, pl.ds(0, h)], y_up)
        for step in (-1, 1, 0):
            shared[step].wait_recv()
            add_into(buf.at[core, at_y(step)], rc.at[at_y(step)])
        yield
        down.wait_recv()
        add_into(buf.at[core, at_y(-1), :, pl.ds(0, h)], rm.at[0, :, pl.ds(0, h)])
        down = send(buf.at[core, at_y(-1)], rm.at[1], y_down)
        up.wait_recv()
        add_into(buf.at[core, at_y(1), :, pl.ds(h, h)], rp.at[0, :, pl.ds(0, h)])
        up = send(buf.at[core, at_y(1)], rp.at[1], y_up)
        yield
        down.wait_recv()
        up.wait_recv()
        theirs = 1 - xlo
        xs_slot[0] = (
            buf[core, y, theirs].astype(F32)
            + rm[1, theirs].astype(F32)
            + rp[1, theirs].astype(F32)
        ).astype(BF16)
        near = send(xs_slot.at[0], rx.at[1], x_near)
        yield
        near.wait_recv()
        out[...] = (
            buf[core, y, xlo].astype(F32)
            + rm[1, xlo].astype(F32)
            + rp[1, xlo].astype(F32)
            + rx[1].astype(F32)
        ).astype(BF16)
        yield

    def taps_sum(flipped, finish):
        def strip_row(bh, carry):
            image, line = bh // 4, bh % 4
            total = jnp.zeros((64, CB), F32)
            for i in range(KS):
                for j in range(KS):
                    tap = dwk[KS - 1 - i, pl.ds(KS - 1 - j, 1)] if flipped else dwk[i, pl.ds(j, 1)]
                    total = total + tap * pad[image, line + i, pl.ds(TAP0 + j, 64)]
            finish(bh, total)
            return carry

        lax.fori_loop(0, 8, strip_row, 0)

    def set_halo(low, high):
        pad[:, 0:3, LEFT : LEFT + 64] = jnp.where(row > 0, low[...].astype(F32), 0.0)
        pad[:, 7:10, LEFT : LEFT + 64] = jnp.where(row < 15, high[...].astype(F32), 0.0)

    lane = lax.broadcasted_iota(jnp.int32, (64, CB), 1)

    def put_sums(bh, first, second):
        tmp[pl.ds(pl.multiple_of(bh * 64, 64), 64)] = jnp.where(
            lane == 0, first, jnp.where(lane == 1, second, 0.0)
        )

    def exchange_sums(slots):
        parts = [jnp.transpose(tmp[q * 128 : (q + 1) * 128]) for q in range(4)]
        slots[col] = jnp.concatenate([p[0:1] for p in parts] + [p[1:2] for p in parts], axis=0)
        return [send(slots.at[col], slots.at[col], col_peer(k)) for k in range(1, 16)]

    def spread(line):
        return jnp.transpose(jnp.broadcast_to(line, (128, 128)))

    copies = [
        send(images.at[:, 1:4], halo_lo, strip_up),
        send(images.at[:, 0:3], halo_hi, strip_down),
    ]
    for q in range(4):
        part = slice(q * 128, (q + 1) * 128)
        gg[z, xhi, part] = (cot[part].astype(F32) * lscale[...]).astype(BF16)
    grads = gather_col(gg)
    next(grads)
    win = gather_row(wi, w_in)
    next(win)
    wout = gather_row(wo, w_out)
    next(wout)

    zero_edge = jnp.zeros((2, 10, LEFT, CB), F32)
    pad[:, :, 0:LEFT] = zero_edge
    pad[:, :, LEFT + 64 : 2 * LEFT + 64] = zero_edge
    pad[:, 3:7, LEFT : LEFT + 64] = images[...].astype(F32)
    for copy in copies:
        copy.wait_recv()
    set_halo(halo_lo, halo_hi)

    def after_conv(bh, total):
        conv[pl.ds(pl.multiple_of(bh * 64, 64), 64)] = total
        mean = jnp.sum(total, axis=1, keepdims=True) * (1.0 / CB)
        dev = total - mean
        put_sums(bh, mean, jnp.sum(dev * dev, axis=1, keepdims=True))

    taps_sum(False, after_conv)
    copies = exchange_sums(st1)
    next(grads)
    next(win)
    next(wout)
    for copy in copies:
        copy.wait_recv()
    stats = st1[...]
    means, devs = stats[:, 0:4], stats[:, 4:8]
    mean = jnp.sum(means, axis=0) * (1.0 / 16)
    off = means - mean[None]
    var = (jnp.sum(devs, axis=0) + CB * jnp.sum(off * off, axis=0)) * (1.0 / C)
    inv = lax.rsqrt(var + 1e-06)
    for q in range(4):
        part = slice(q * 128, (q + 1) * 128)
        scale = spread(inv[q : q + 1])
        value = (conv[part] - spread(mean[q : q + 1])) * scale
        istd[part] = scale
        normed[part] = value
        xg[z, xhi, part] = (value * gain[...]).astype(BF16)
    pix = gather_col(xg)
    next(pix)

    def pair(buf, zi):
        return jnp.concatenate([buf[zi, 0], buf[zi, 1]], axis=1)

    def panel(buf, zi):
        xi, yi = zi // NY, zi % NY
        return jnp.concatenate([buf[0, yi, xi], buf[1, yi, xi]], axis=0)

    def product(acc, buf, weight, step, first):
        zi = at_z(step)
        term = jnp.dot(pair(buf, zi), panel(weight, zi), preferred_element_type=F32)
        if first:
            acc[...] = term
        else:
            acc[...] += term

    next(grads)
    next(win)
    next(wout)
    next(pix)
    next(grads)
    next(win)
    next(wout)
    next(pix)
    next(grads)
    next(win)
    next(wout)
    next(pix)
    next(win)
    next(wout)
    next(grads)
    next(pix)
    next(grads)
    product(gh, gg, wo, 0, True)
    for step in (1, -1, 2, -2, 3, -3, 4):
        product(gh, gg, wo, step, False)
    product(hp, xg, wi, 0, True)
    for step in (1, -1, 2, -2):
        product(hp, xg, wi, step, False)
    next(pix)
    next(pix)
    for step in (3, -3, 4):
        product(hp, xg, wi, step, False)

    def activate(i, carry):
        part = pl.ds(pl.multiple_of(i * 64, 64), 64)
        v = hp[part]
        cdf = 0.5 * (1.0 + lax.erf(v * 0.7071067811865476))
        slope = cdf + v * jnp.exp(-0.5 * v * v) * 0.3989422804014327
        hid[part] = (v * cdf).astype(BF16)
        gpre[part] = (gh[part] * slope).astype(BF16)
        return carry

    lax.fori_loop(0, 8, activate, 0)

    def to_channels(dst, act, weight, step):
        zi = at_z(step)
        term = lax.dot_general(
            act[...], panel(weight, zi), CONTRACT_LAST, preferred_element_type=F32
        ).astype(BF16)
        dst[zi, 0] = term[:, 0:CB]
        dst[zi, 1] = term[:, CB : 2 * CB]

    order = (4, -3, 3, -2, 2, -1, 1, 0)
    for step in order:
        to_channels(bk, gpre, wi, step)
    back = scatter_col(bk, bk_m, bk_p, bk_m1, bk_p1, bk_x, bk_xs, bk_xr, gs)
    next(back)

    def weight_grad(dst, buf, act):
        def one(zi, carry):
            xi, yi = zi // NY, zi % NY
            term = lax.dot_general(
                pair(buf, zi), act[...], CONTRACT_FIRST, preferred_element_type=F32
            ).astype(BF16)
            dst[0, yi, xi] = term[0:CB]
            dst[1, yi, xi] = term[CB : 2 * CB]
            return carry

        lax.fori_loop(0, NZ, one, 0)

    weight_grad(g2, gg, hid)
    sum2 = scatter_row(g2, g2_c, g2_m, g2_p, g2_r, g2_r, gp_out)
    next(sum2)
    next(back)
    weight_grad(g1, xg, gpre)
    sum1 = scatter_row(g1, g1_c, g1_m, g1_p, g1_r, g1_r, gp_in)
    next(sum1)
    next(back)
    for step in order:
        to_channels(cb, hid, wo, step)
    next(sum2)
    next(back)
    branch = scatter_col(cb, cb_m, cb_p, cb_m1, cb_p1, cb_x, cb_xs, cb_xr, hp.at[:, 0:CB])
    next(branch)
    next(sum1)
    next(sum2)
    next(back)
    next(back)

    def sums(bh, carry):
        part = pl.ds(pl.multiple_of(bh * 64, 64), 64)
        weighted = gs[part] * gain[...]
        gs[part] = weighted
        put_sums(
            bh,
            jnp.sum(weighted, axis=1, keepdims=True),
            jnp.sum(weighted * normed[part], axis=1, keepdims=True),
        )
        return carry

    lax.fori_loop(0, 8, sums, 0)
    copies = exchange_sums(st2)
    next(branch)
    next(sum1)
    next(sum2)
    for copy in copies:
        copy.wait_recv()
    total = jnp.sum(st2[...], axis=0) * (1.0 / C)
    for q in range(4):
        part = slice(q * 128, (q + 1) * 128)
        value = istd[part] * (
            gs[part] - spread(total[q : q + 1]) - normed[part] * spread(total[4 + q : 5 + q])
        )
        image, line = q // 2, 2 * (q % 2)
        value = value.reshape(2, 64, CB)
        pad[image, 3 + line : 5 + line, LEFT : LEFT + 64] = value
        value = value.astype(BF16)
        if line == 0:
            edge_hi[image, 0:2] = value
            edge_lo[image, 0:1] = value[1:2]
        else:
            edge_hi[image, 2:3] = value[0:1]
            edge_lo[image, 1:3] = value
    copies = [send(edge_lo, ghalo_lo, strip_up), send(edge_hi, ghalo_hi, strip_down)]
    next(branch)
    next(sum1)
    next(sum2)
    for copy in copies:
        copy.wait_recv()
    set_halo(ghalo_lo, ghalo_hi)

    def after_transposed(bh, total):
        part = pl.ds(pl.multiple_of(bh * 64, 64), 64)
        grad_images[bh // 4, bh % 4] = (cot[part].astype(F32) + total).astype(BF16)

    taps_sum(True, after_transposed)

    next(sum1)
    next(branch)
    next(branch)
    next(branch)
    branch_sum = hp.at[:, 0:CB]
    for q in range(8):
        part = slice(q * 64, (q + 1) * 64)
        image, line = q // 4, q % 4
        block_out[image, line] = (
            images[image, line].astype(F32) + lscale[...] * branch_sum[part]
        ).astype(BF16)
    for copy in started:
        copy.wait_send()


def on_device(images, dw_kernel, norm_gain, proj_in, proj_out, layer_scale, cotangent):
    n0 = 512
    n1 = PIX - n0
    a0, a1 = max(n0, 16), max(n1, 16)
    strip = images.shape
    vmem = pltpu.VMEM
    col_blocks = vmem((NZ, 2, PIX, CB), BF16)
    row_blocks = vmem((2, NY, 2, CB, HB), BF16)
    scratch = (
        [vmem((2, 10, 64 + 2 * LEFT, CB), F32)]
        + [vmem((2, 3, 64, CB), BF16)] * 6
        + [vmem((PIX, CB), F32)] * 4
        + [vmem((16, 8, CB), F32)] * 2
        + [col_blocks] * 2
        + [row_blocks] * 2
        + [vmem((PIX, HB), F32)] * 2
        + [vmem((PIX, HB), BF16)] * 2
        + [col_blocks] * 2
        + [vmem((4, 2, a0, CB), BF16)] * 4
        + [vmem((4, a1, CB), BF16)] * 4
        + [vmem((NZ, a1, CB), BF16)] * 2
        + [vmem((a0, CB), BF16)] * 4
        + [vmem((PIX, CB), F32)]
        + [row_blocks] * 2
        + [vmem((NY, 2, CB, HB), BF16)] * 2
        + [vmem((2, 2, CB, HB), BF16)] * 4
        + [vmem((2, CB, HB), BF16)] * 2
        + [pltpu.SemaphoreType.DMA((N_SEMS,))] * 2
    )
    block = pl.BlockSpec(memory_space=pltpu.VMEM)
    return pl.pallas_call(
        functools.partial(kernel, n0),
        out_shape=(
            jax.ShapeDtypeStruct(strip, BF16),
            jax.ShapeDtypeStruct(strip, BF16),
            jax.ShapeDtypeStruct(proj_in.shape, BF16),
            jax.ShapeDtypeStruct(proj_out.shape, BF16),
        ),
        in_specs=[block] * 7,
        out_specs=(block,) * 4,
        scratch_shapes=scratch,
        compiler_params=pltpu.CompilerParams(
            collective_id=0, has_side_effects=True, vmem_limit_bytes=56 << 20
        ),
    )(
        images,
        dw_kernel,
        norm_gain.reshape(1, CB),
        proj_in,
        proj_out,
        layer_scale.reshape(1, CB),
        cotangent.reshape(PIX, CB),
    )


def solution(mesh):
    placed = (
        P(None, "row", None, "col"),
        P(None, None, "col"),
        P("col"),
        P("row", "col"),
        P("row", "col"),
        P("col"),
        P(None, "row", None, "col"),
    )
    return jax.shard_map(
        on_device,
        mesh=mesh,
        in_specs=placed,
        out_specs=(
            P(None, "row", None, "col"),
            P(None, "row", None, "col"),
            P("row", "col"),
            P("row", "col"),
        ),
        check_vma=False,
    )
```

```python
import functools

import jax
import jax.numpy as jnp
from jax import lax
from jax.experimental import pallas as pl
from jax.experimental.pallas import tpu as pltpu
from jax.sharding import PartitionSpec as P

MESH = pl.DeviceIdType.MESH
F32, BF16 = jnp.float32, jnp.bfloat16
C = 2048
KS = 7
NZ, NY = 8, 4
CB = 128
HB = 512
PIX = 512
LEFT = 8
TAP0 = LEFT - KS // 2
N_SEMS = 256
CONTRACT_LAST = (((1,), (1,)), ((), ()))
CONTRACT_FIRST = (((0,), (0,)), ((), ()))


def kernel(
    n0,
    images, dwk, gain, w_in, w_out, lscale, cot,
    block_out, grad_images, gp_in, gp_out,
    pad, halo_lo, halo_hi, ghalo_lo, ghalo_hi, edge_lo, edge_hi,
    conv, normed, istd, tmp, st1, st2,
    cols, xg, xs, gg, wi, wo, hp, gh, hid, gpre,
    cb, bk, cb_m, cb_p, bk_m, bk_p, cb_m1, cb_p1, bk_m1, bk_p1,
    cb_x, bk_x, cb_xs, bk_xs, cb_xr, bk_xr, gs,
    g1, g2, g1_c, g2_c, g1_m, g1_p, g2_m, g2_p, g1_r, g2_r,
    send_sem, recv_sem,
):
    n1 = PIX - n0
    row, col = lax.axis_index("row"), lax.axis_index("col")
    xlo, y, core = row // 8, (row // 2) % NY, row % 2
    z, xhi = col // 2, col % 2

    def at_z(step):
        return (z + step + NZ) % NZ

    def at_y(step):
        return (y + step + NY) % NY

    z_up = {"row": row, "col": at_z(1) * 2 + xhi}
    z_down = {"row": row, "col": at_z(-1) * 2 + xhi}
    x_far = {"row": row, "col": z * 2 + (1 - xhi)}
    y_up = {"row": xlo * 8 + at_y(1) * 2 + core, "col": col}
    y_down = {"row": xlo * 8 + at_y(-1) * 2 + core, "col": col}
    x_near = {"row": (1 - xlo) * 8 + y * 2 + core, "col": col}
    sibling = {"row": xlo * 8 + y * 2 + (1 - core), "col": col}
    strip_up = {"row": (row + 1) % 16, "col": col}
    strip_down = {"row": (row + 15) % 16, "col": col}

    def col_peer(step):
        return {"row": row, "col": (col + step) % 16}

    started = []

    def send(src, dst, where):
        index = len(started)
        copy = pltpu.make_async_remote_copy(
            src_ref=src, dst_ref=dst, send_sem=send_sem.at[index], recv_sem=recv_sem.at[index],
            device_id=where, device_id_type=MESH,
        )
        copy.start()
        started.append(copy)
        return copy

    zero_edge = jnp.zeros((2, 10, LEFT, CB), F32)
    pad[:, :, 0:LEFT] = zero_edge
    pad[:, :, LEFT + 64 : 2 * LEFT + 64] = zero_edge
    pad[:, 3:7, LEFT : LEFT + 64] = images[...].astype(F32)
    for q in range(4):
        part = slice(q * 128, (q + 1) * 128)
        gg[z, xhi, part] = (cot[part].astype(F32) * lscale[...]).astype(BF16)
    wi[core, y, xlo] = w_in[...]
    wo[core, y, xlo] = w_out[...]

    barrier = pltpu.get_barrier_semaphore()
    peers = [strip_up, strip_down, y_up, y_down, x_near, x_far, z_up, z_down]
    for peer in peers:
        pl.semaphore_signal(barrier, inc=1, device_id=peer, device_id_type=MESH)
    pl.semaphore_wait(barrier, len(peers))

    def ring_gather(buf, half, first, count):
        def block(zi, lo=0, n=count):
            return buf.at[zi, half, pl.ds(first + lo, n)]
        up = send(block(z), block(z), z_up)
        down = send(block(z), block(z), z_down)
        yield
        for k in (1, 2, 3):
            up.wait_recv()
            down.wait_recv()
            if k < 3:
                up = send(block(at_z(-k)), block(at_z(-k)), z_up)
                down = send(block(at_z(k)), block(at_z(k)), z_down)
            else:
                h = count // 2
                up = send(block(at_z(-3), 0, h), block(at_z(-3), 0, h), z_up)
                down = send(block(at_z(3), h, h), block(at_z(3), h, h), z_down)
            yield
        up.wait_recv()
        down.wait_recv()
        yield

    def gather_col(buf):
        def rows(zi, half, first, count):
            return buf.at[zi, half, pl.ds(first, count)]

        far = {k: [] for k in range(5)}
        rings = []
        if n0:
            near = send(rows(z, xhi, 0, n0), rows(z, xhi, 0, n0), x_far)
            rings.append(ring_gather(buf, xhi, 0, n0))
        if n1:
            rings.append(ring_gather(buf, xhi, n0, n1))
        for ring in rings:
            next(ring)
        if n1:
            far[0].append(send(rows(z, xhi, n0, n1), rows(z, xhi, n0, n1), x_far))
        yield
        late = ring_gather(buf, 1 - xhi, 0, n0)
        for k in (1, 2, 3, 4, 5):
            if k < 5:
                for ring in rings:
                    next(ring)
                if n1:
                    for step in sorted({-k, k} if k < 4 else {4}):
                        part = rows(at_z(step), xhi, n0, n1)
                        far[k].append(send(part, part, x_far))
            if n0:
                if k == 1:
                    near.wait_recv()
                next(late)
            for i in {1: (), 2: (0,), 3: (1,), 4: (2,), 5: (3, 4)}[k]:
                for copy in far[i]:
                    copy.wait_recv()
            yield

    def gather_stats(slots):
        near = send(slots.at[0, 0], slots.at[0, 1], x_far)
        yield
        near.wait_recv()
        up = send(slots.at[0], slots.at[NZ - 1], z_up)
        down = send(slots.at[0], slots.at[1], z_down)
        yield
        for k in (1, 2, 3):
            up.wait_recv()
            up = send(slots.at[NZ - k], slots.at[NZ - k - 1], z_up)
            down.wait_recv()
            if k < 3:
                down = send(slots.at[k], slots.at[k + 1], z_down)
            yield
        up.wait_recv()
        yield

    def gather_row(buf, own):
        def block(k, yi, xi, lo=0, n=CB):
            return buf.at[k, yi, xi, pl.ds(lo, n)]
        waits = []

        def share(yi, xi):
            waits.append(send(block(core, yi, xi), block(core, yi, xi), sibling))

        near = send(own, block(core, y, xlo), x_near)
        up, down = {}, {}
        up[0] = send(own, block(core, y, xlo), y_up)
        down[0] = send(own, block(core, y, xlo), y_down)
        waits.append(send(own, block(core, y, xlo), sibling))
        yield
        near.wait_recv()
        other = 1 - xlo
        up[1] = send(block(core, y, other), block(core, y, other), y_up)
        down[1] = send(block(core, y, other), block(core, y, other), y_down)
        share(y, other)
        yield
        h = CB // 2
        for i, xi in enumerate((xlo, other)):
            up[i].wait_recv()
            down[i].wait_recv()
            low, high = block(core, at_y(-1), xi, 0, h), block(core, at_y(1), xi, h, h)
            up[i] = send(low, low, y_up)
            down[i] = send(high, high, y_down)
            share(at_y(-1), xi)
            share(at_y(1), xi)
            yield
        for i, xi in enumerate((xlo, other)):
            up[i].wait_recv()
            down[i].wait_recv()
            share(at_y(2), xi)
        yield
        for copy in waits:
            copy.wait_recv()
        yield

    def add_into(dst, src):
        dst[...] = (dst[...].astype(F32) + src[...].astype(F32)).astype(BF16)

    def scatter_col(buf, rm, rp, rm1, rp1, rx1, xs, xr, total):
        h0, h1 = n0 // 2, n1 // 2
        if n1:
            first = {}
            for step in (4, -3, 3, -2, 2, -1, 1, 0):
                first[step] = send(
                    buf.at[at_z(step), 1 - xhi, pl.ds(n0, n1)], rx1.at[at_z(step)], x_far
                )
        copies = {}

        def block0(zi, lo=0, n=n0):
            return buf.at[zi, :, pl.ds(lo, n)]

        def block1(zi, lo=0, n=n1):
            return buf.at[zi, xhi, pl.ds(n0 + lo, n)]

        for k in (1, 2, 3, 4):
            dist = 5 - k
            if n0:
                if k == 1:
                    down = send(block0(at_z(-4), 0, h0), rm.at[0, :, pl.ds(0, h0)], z_down)
                    up = send(block0(at_z(4), h0, h0), rp.at[0, :, pl.ds(0, h0)], z_up)
                else:
                    down.wait_recv()
                    if k == 2:
                        add_into(block0(at_z(-dist), 0, h0), rm.at[0, :, pl.ds(0, h0)])
                    else:
                        add_into(block0(at_z(-dist)), rm.at[k - 2])
                    down = send(block0(at_z(-dist)), rm.at[k - 1], z_down)
                    up.wait_recv()
                    if k == 2:
                        add_into(block0(at_z(dist), h0, h0), rp.at[0, :, pl.ds(0, h0)])
                    else:
                        add_into(block0(at_z(dist)), rp.at[k - 2])
                    up = send(block0(at_z(dist)), rp.at[k - 1], z_up)
            if n1:
                if k == 1:
                    first[4].wait_recv()
                    add_into(block1(at_z(4)), rx1.at[at_z(4)])
                    down1 = send(block1(at_z(-4), 0, h1), rm1.at[0, pl.ds(0, h1)], z_down)
                    up1 = send(block1(at_z(4), h1, h1), rp1.at[0, pl.ds(0, h1)], z_up)
                else:
                    first[-dist].wait_recv()
                    add_into(block1(at_z(-dist)), rx1.at[at_z(-dist)])
                    first[dist].wait_recv()
                    add_into(block1(at_z(dist)), rx1.at[at_z(dist)])
                    down1.wait_recv()
                    if k == 2:
                        add_into(block1(at_z(-dist), 0, h1), rm1.at[0, pl.ds(0, h1)])
                    else:
                        add_into(block1(at_z(-dist)), rm1.at[k - 2])
                    down1 = send(block1(at_z(-dist)), rm1.at[k - 1], z_down)
                    up1.wait_recv()
                    if k == 2:
                        add_into(block1(at_z(dist), h1, h1), rp1.at[0, pl.ds(0, h1)])
                    else:
                        add_into(block1(at_z(dist)), rp1.at[k - 2])
                    up1 = send(block1(at_z(dist)), rp1.at[k - 1], z_up)
            yield
        if n0:
            down.wait_recv()
            up.wait_recv()
            theirs = 1 - xhi
            xs[...] = (
                buf[z, theirs, 0:n0].astype(F32)
                + rm[3, theirs].astype(F32)
                + rp[3, theirs].astype(F32)
            ).astype(BF16)
            far = send(xs, xr, x_far)
        if n1:
            first[0].wait_recv()
            down1.wait_recv()
            up1.wait_recv()
            total[n0:PIX] = (
                buf[z, xhi, n0:PIX].astype(F32)
                + rx1[z].astype(F32)
                + rm1[3].astype(F32)
                + rp1[3].astype(F32)
            )
        yield
        if n0:
            far.wait_recv()
            total[0:n0] = (
                buf[z, xhi, 0:n0].astype(F32)
                + rm[3, xhi].astype(F32)
                + rp[3, xhi].astype(F32)
                + xr[...].astype(F32)
            )
        yield

    def scatter_row(buf, rc, rm, rp, rx, xs_slot, out):
        h = CB // 2
        shared = {}
        for step in (2, -1, 1, 0):
            shared[step] = send(buf.at[1 - core, at_y(step)], rc.at[at_y(step)], sibling)
        yield
        shared[2].wait_recv()
        add_into(buf.at[core, at_y(2)], rc.at[at_y(2)])
        down = send(
            buf.at[core, at_y(-2), :, pl.ds(0, h)], rm.at[0, :, pl.ds(0, h)], y_down
        )
        up = send(buf.at[core, at_y(2), :, pl.ds(h, h)], rp.at[0, :, pl.ds(0, h)], y_up)
        for step in (-1, 1, 0):
            shared[step].wait_recv()
            add_into(buf.at[core, at_y(step)], rc.at[at_y(step)])
        yield
        down.wait_recv()
        add_into(buf.at[core, at_y(-1), :, pl.ds(0, h)], rm.at[0, :, pl.ds(0, h)])
        down = send(buf.at[core, at_y(-1)], rm.at[1], y_down)
        up.wait_recv()
        add_into(buf.at[core, at_y(1), :, pl.ds(h, h)], rp.at[0, :, pl.ds(0, h)])
        up = send(buf.at[core, at_y(1)], rp.at[1], y_up)
        yield
        down.wait_recv()
        up.wait_recv()
        theirs = 1 - xlo
        xs_slot[0] = (
            buf[core, y, theirs].astype(F32)
            + rm[1, theirs].astype(F32)
            + rp[1, theirs].astype(F32)
        ).astype(BF16)
        near = send(xs_slot.at[0], rx.at[1], x_near)
        yield
        near.wait_recv()
        out[...] = (
            buf[core, y, xlo].astype(F32)
            + rm[1, xlo].astype(F32)
            + rp[1, xlo].astype(F32)
            + rx[1].astype(F32)
        ).astype(BF16)
        yield

    def taps_sum(flipped, finish):
        def strip_row(bh, carry):
            image, line = bh // 4, bh % 4
            total = jnp.zeros((64, CB), F32)
            for i in range(KS):
                for j in range(KS):
                    tap = dwk[KS - 1 - i, pl.ds(KS - 1 - j, 1)] if flipped else dwk[i, pl.ds(j, 1)]
                    total = total + tap * pad[image, line + i, pl.ds(TAP0 + j, 64)]
            finish(bh, total)
            return carry

        lax.fori_loop(0, 8, strip_row, 0)

    def set_halo(low, high):
        pad[:, 0:3, LEFT : LEFT + 64] = jnp.where(row > 0, low[...].astype(F32), 0.0)
        pad[:, 7:10, LEFT : LEFT + 64] = jnp.where(row < 15, high[...].astype(F32), 0.0)

    lane = lax.broadcasted_iota(jnp.int32, (64, CB), 1)

    def put_sums(bh, first, second):
        tmp[pl.ds(pl.multiple_of(bh * 64, 64), 64)] = jnp.where(
            lane == 0, first, jnp.where(lane == 1, second, 0.0)
        )

    def packed_sums():
        parts = [jnp.transpose(tmp[q * 128 : (q + 1) * 128]) for q in range(4)]
        return jnp.concatenate([p[0:1] for p in parts] + [p[1:2] for p in parts], axis=0)

    def exchange_sums(slots):
        slots[col] = packed_sums()
        return [send(slots.at[col], slots.at[col], col_peer(k)) for k in range(1, 16)]

    def spread(line):
        return jnp.transpose(jnp.broadcast_to(line, (128, 128)))

    copies = [
        send(images.at[:, 1:4], halo_lo, strip_up),
        send(images.at[:, 0:3], halo_hi, strip_down),
    ]
    grads = gather_col(gg)
    next(grads)
    win = gather_row(wi, w_in)
    next(win)
    wout = gather_row(wo, w_out)
    next(wout)

    for copy in copies:
        copy.wait_recv()
    set_halo(halo_lo, halo_hi)

    def after_conv(bh, total):
        part = pl.ds(pl.multiple_of(bh * 64, 64), 64)
        conv[part] = total
        mean = jnp.sum(total, axis=1, keepdims=True) * (1.0 / CB)
        dev = total - mean
        xg[z, xhi, part] = dev.astype(BF16)
        put_sums(bh, mean, jnp.sum(dev * dev, axis=1, keepdims=True))

    taps_sum(False, after_conv)
    pix = gather_col(xg)
    next(pix)
    st1[0, 0, 0:8] = packed_sums()
    st1[0, 0, 8:16] = jnp.broadcast_to(gain[...], (8, CB))
    stats = gather_stats(st1)
    next(stats)

    def pair(buf, zi):
        return jnp.concatenate([buf[zi, 0], buf[zi, 1]], axis=1)

    def panel(buf, zi):
        xi, yi = zi // NY, zi % NY
        return jnp.concatenate([buf[0, yi, xi], buf[1, yi, xi]], axis=0)

    def product(acc, buf, weight, step, first):
        zi = at_z(step)
        term = jnp.dot(pair(buf, zi), panel(weight, zi), preferred_element_type=F32)
        if first:
            acc[...] = term
        else:
            acc[...] += term

    def normalise(step):
        for other in (0, 1):
            slot = (step % NZ, other)
            half = xhi if other == 0 else 1 - xhi
            place = slot[0] * 2 + other
            scale = st1[slot[0], other, 8:9]
            for q in range(4):
                part = slice(q * 128, (q + 1) * 128)
                dev = xg[at_z(step), half, part].astype(F32)
                value = (dev + cols[q, :, place : place + 1]) * istd[part] * scale
                xs[at_z(step), half, part] = value.astype(BF16)

    next(grads)
    next(win)
    next(wout)
    next(pix)
    next(stats)
    next(grads)
    next(win)
    next(wout)
    next(stats)
    next(pix)
    next(grads)
    next(win)
    next(wout)
    next(stats)
    next(pix)
    next(grads)
    next(win)
    next(wout)
    next(stats)
    next(pix)
    next(grads)
    next(win)
    next(wout)
    next(stats)
    every = st1[...]
    means, devs = every[:, :, 0:4], every[:, :, 4:8]
    mean = jnp.sum(means, axis=(0, 1)) * (1.0 / 16)
    shift = means - mean[None, None]
    var = (jnp.sum(devs, axis=(0, 1)) + CB * jnp.sum(shift * shift, axis=(0, 1))) * (1.0 / C)
    inv = lax.rsqrt(var + 1e-06)
    for q in range(4):
        part = slice(q * 128, (q + 1) * 128)
        lines = [shift[o, i, q : q + 1] for o in range(NZ) for i in range(2)]
        lines += [inv[q : q + 1], mean[q : q + 1], jnp.zeros((110, 128), F32)]
        turned = jnp.transpose(jnp.concatenate(lines, axis=0))
        cols[q] = turned
        scale = jnp.broadcast_to(turned[:, 16:17], (128, CB))
        istd[part] = scale
        normed[part] = (conv[part] - turned[:, 17:18]) * scale
    product(gh, gg, wo, 0, True)
    for step in (1, -1, 2, -2, 3, -3, 4):
        product(gh, gg, wo, step, False)
    for step in (0, 1, -1, 2, -2):
        normalise(step)
        product(hp, xs, wi, step, step == 0)
    next(pix)
    for step in (3, -3, 4):
        normalise(step)
        product(hp, xs, wi, step, False)

    def activate(i, carry):
        part = pl.ds(pl.multiple_of(i * 64, 64), 64)
        v = hp[part]
        cdf = 0.5 * (1.0 + lax.erf(v * 0.7071067811865476))
        slope = cdf + v * jnp.exp(-0.5 * v * v) * 0.3989422804014327
        hid[part] = (v * cdf).astype(BF16)
        gpre[part] = (gh[part] * slope).astype(BF16)
        return carry

    lax.fori_loop(0, 8, activate, 0)

    def to_channels(dst, act, weight, step):
        zi = at_z(step)
        term = lax.dot_general(
            act[...], panel(weight, zi), CONTRACT_LAST, preferred_element_type=F32
        ).astype(BF16)
        dst[zi, 0] = term[:, 0:CB]
        dst[zi, 1] = term[:, CB : 2 * CB]

    order = (4, -3, 3, -2, 2, -1, 1, 0)
    for step in order:
        to_channels(bk, gpre, wi, step)
    back = scatter_col(bk, bk_m, bk_p, bk_m1, bk_p1, bk_x, bk_xs, bk_xr, gs)
    next(back)

    def weight_grad(dst, buf, act):
        def one(zi, carry):
            xi, yi = zi // NY, zi % NY
            term = lax.dot_general(
                pair(buf, zi), act[...], CONTRACT_FIRST, preferred_element_type=F32
            ).astype(BF16)
            dst[0, yi, xi] = term[0:CB]
            dst[1, yi, xi] = term[CB : 2 * CB]
            return carry

        lax.fori_loop(0, NZ, one, 0)

    weight_grad(g2, gg, hid)
    sum2 = scatter_row(g2, g2_c, g2_m, g2_p, g2_r, g2_r, gp_out)
    next(sum2)
    next(back)
    weight_grad(g1, xs, gpre)
    sum1 = scatter_row(g1, g1_c, g1_m, g1_p, g1_r, g1_r, gp_in)
    next(sum1)
    next(back)
    for step in order:
        to_channels(cb, hid, wo, step)
    next(sum2)
    next(back)
    branch = scatter_col(cb, cb_m, cb_p, cb_m1, cb_p1, cb_x, cb_xs, cb_xr, hp.at[:, 0:CB])
    next(branch)
    next(sum1)
    next(sum2)
    next(back)
    next(back)

    def sums(bh, carry):
        part = pl.ds(pl.multiple_of(bh * 64, 64), 64)
        weighted = gs[part] * gain[...]
        gs[part] = weighted
        put_sums(
            bh,
            jnp.sum(weighted, axis=1, keepdims=True),
            jnp.sum(weighted * normed[part], axis=1, keepdims=True),
        )
        return carry

    lax.fori_loop(0, 8, sums, 0)
    copies = exchange_sums(st2)
    next(branch)
    next(sum1)
    next(sum2)
    for copy in copies:
        copy.wait_recv()
    total = jnp.sum(st2[...], axis=0) * (1.0 / C)
    for q in range(4):
        part = slice(q * 128, (q + 1) * 128)
        value = istd[part] * (
            gs[part] - spread(total[q : q + 1]) - normed[part] * spread(total[4 + q : 5 + q])
        )
        image, line = q // 2, 2 * (q % 2)
        value = value.reshape(2, 64, CB)
        pad[image, 3 + line : 5 + line, LEFT : LEFT + 64] = value
        value = value.astype(BF16)
        if line == 0:
            edge_hi[image, 0:2] = value
            edge_lo[image, 0:1] = value[1:2]
        else:
            edge_hi[image, 2:3] = value[0:1]
            edge_lo[image, 1:3] = value
    copies = [send(edge_lo, ghalo_lo, strip_up), send(edge_hi, ghalo_hi, strip_down)]
    next(branch)
    next(sum1)
    next(sum2)
    for copy in copies:
        copy.wait_recv()
    set_halo(ghalo_lo, ghalo_hi)

    def after_transposed(bh, total):
        part = pl.ds(pl.multiple_of(bh * 64, 64), 64)
        grad_images[bh // 4, bh % 4] = (cot[part].astype(F32) + total).astype(BF16)

    taps_sum(True, after_transposed)

    next(sum1)
    next(branch)
    next(branch)
    next(branch)
    branch_sum = hp.at[:, 0:CB]
    for q in range(8):
        part = slice(q * 64, (q + 1) * 64)
        image, line = q // 4, q % 4
        block_out[image, line] = (
            images[image, line].astype(F32) + lscale[...] * branch_sum[part]
        ).astype(BF16)
    for copy in started:
        copy.wait_send()


def on_device(images, dw_kernel, norm_gain, proj_in, proj_out, layer_scale, cotangent):
    n0 = 256
    n1 = PIX - n0
    a0, a1 = max(n0, 16), max(n1, 16)
    strip = images.shape
    vmem = pltpu.VMEM
    col_blocks = vmem((NZ, 2, PIX, CB), BF16)
    row_blocks = vmem((2, NY, 2, CB, HB), BF16)
    scratch = (
        [vmem((2, 10, 64 + 2 * LEFT, CB), F32)]
        + [vmem((2, 3, 64, CB), BF16)] * 6
        + [vmem((PIX, CB), F32)] * 4
        + [vmem((NZ, 2, 16, CB), F32), vmem((16, 8, CB), F32), vmem((4, 128, 128), F32)]
        + [col_blocks] * 3
        + [row_blocks] * 2
        + [vmem((PIX, HB), F32)] * 2
        + [vmem((PIX, HB), BF16)] * 2
        + [col_blocks] * 2
        + [vmem((4, 2, a0, CB), BF16)] * 4
        + [vmem((4, a1, CB), BF16)] * 4
        + [vmem((NZ, a1, CB), BF16)] * 2
        + [vmem((a0, CB), BF16)] * 4
        + [vmem((PIX, CB), F32)]
        + [row_blocks] * 2
        + [vmem((NY, 2, CB, HB), BF16)] * 2
        + [vmem((2, 2, CB, HB), BF16)] * 4
        + [vmem((2, CB, HB), BF16)] * 2
        + [pltpu.SemaphoreType.DMA((N_SEMS,))] * 2
    )
    block = pl.BlockSpec(memory_space=pltpu.VMEM)
    return pl.pallas_call(
        functools.partial(kernel, n0),
        out_shape=(
            jax.ShapeDtypeStruct(strip, BF16),
            jax.ShapeDtypeStruct(strip, BF16),
            jax.ShapeDtypeStruct(proj_in.shape, BF16),
            jax.ShapeDtypeStruct(proj_out.shape, BF16),
        ),
        in_specs=[block] * 7,
        out_specs=(block,) * 4,
        scratch_shapes=scratch,
        compiler_params=pltpu.CompilerParams(
            collective_id=0, has_side_effects=True, vmem_limit_bytes=56 << 20
        ),
    )(
        images,
        dw_kernel,
        norm_gain.reshape(1, CB),
        proj_in,
        proj_out,
        layer_scale.reshape(1, CB),
        cotangent.reshape(PIX, CB),
    )


def solution(mesh):
    placed = (
        P(None, "row", None, "col"),
        P(None, None, "col"),
        P("col"),
        P("row", "col"),
        P("row", "col"),
        P("col"),
        P(None, "row", None, "col"),
    )
    return jax.shard_map(
        on_device,
        mesh=mesh,
        in_specs=placed,
        out_specs=(
            P(None, "row", None, "col"),
            P(None, "row", None, "col"),
            P("row", "col"),
            P("row", "col"),
        ),
        check_vma=False,
    )
```

```python
import functools

import jax
import jax.numpy as jnp
from jax import lax
from jax.experimental import pallas as pl
from jax.experimental.pallas import tpu as pltpu
from jax.sharding import PartitionSpec as P

MESH = pl.DeviceIdType.MESH
F32, BF16 = jnp.float32, jnp.bfloat16
C = 2048
KS = 7
NZ, NY = 8, 4
CB = 128
HB = 512
PIX = 512
LEFT = 8
TAP0 = LEFT - KS // 2
N_SEND, N_RECV = 21, 165
GATHER_ORDER = "gGWwxXSgGWwSxXgGWwSxXgGWwSxXgWwSx"
BACK_ORDER = "mMBknNbBMcCbBNcCbBMcCbBNB"
HALO_ORDER = "McCN"
LAST_ORDER = "MNCC"
CONTRACT_LAST = (((1,), (1,)), ((), ()))
CONTRACT_FIRST = (((0,), (0,)), ((), ()))


def kernel(
    n0,
    images, dwk, gain, w_in, w_out, lscale, cot,
    block_out, grad_images, gp_in, gp_out,
    pad, halo_lo, halo_hi, ghalo_lo, ghalo_hi, edge_lo, edge_hi,
    conv, normed, istd, tmp, st1, st2,
    cols, xg, xs, gg, wi, wo, hp, gh, hid, gpre,
    gw, cb, bk, cb_m, cb_p, bk_m, bk_p, cb_mo, cb_po, bk_mo, bk_po,
    cb_x, bk_x, cb_xs, bk_xs, cb_xr, bk_xr, gs,
    g1, g2, g1_c, g2_c, g1_m, g1_p, g2_m, g2_p, g1_r, g2_r,
    send_sem, recv_sem,
):
    n1 = PIX - n0
    row, col = lax.axis_index("row"), lax.axis_index("col")
    xlo, y, core = row // 8, (row // 2) % NY, row % 2
    z, xhi = col // 2, col % 2

    def at_z(step):
        return (z + step + NZ) % NZ

    def at_y(step):
        return (y + step + NY) % NY

    z_up = {"row": row, "col": at_z(1) * 2 + xhi}
    z_down = {"row": row, "col": at_z(-1) * 2 + xhi}
    x_far = {"row": row, "col": z * 2 + (1 - xhi)}
    y_up = {"row": xlo * 8 + at_y(1) * 2 + core, "col": col}
    y_down = {"row": xlo * 8 + at_y(-1) * 2 + core, "col": col}
    x_near = {"row": (1 - xlo) * 8 + y * 2 + core, "col": col}
    sibling = {"row": xlo * 8 + y * 2 + (1 - core), "col": col}
    strip_up = {"row": (row + 1) % 16, "col": col}
    strip_down = {"row": (row + 15) % 16, "col": col}

    def col_peer(step):
        return {"row": row, "col": (col + step) % 16}

    counts = {"recv": 0, "send": 0}

    def take(kind):
        counts[kind] += 1
        return counts[kind] - 1

    sends = []

    def group(whole):
        sends.append((take("send"), whole))
        return sends[-1][0]

    def send(src, dst, where, sem=None, recv=None):
        if sem is None:
            sem = group(src)
        copy = pltpu.make_async_remote_copy(
            src_ref=src, dst_ref=dst, send_sem=send_sem.at[sem],
            recv_sem=recv_sem.at[take("recv") if recv is None else recv],
            device_id=where, device_id_type=MESH,
        )
        copy.start()
        return copy

    def blocks15():
        return group(xg.at[0:15])

    zero_edge = jnp.zeros((2, 10, LEFT, CB), F32)
    pad[:, :, 0:LEFT] = zero_edge
    pad[:, :, LEFT + 64 : 2 * LEFT + 64] = zero_edge
    pad[:, 3:7, LEFT : LEFT + 64] = images[...].astype(F32)
    for q in range(4):
        part = slice(q * 128, (q + 1) * 128)
        gg[col, part] = (cot[part].astype(F32) * lscale[...]).astype(BF16)
    wi[core, y, xlo] = w_in[...]
    wo[core, y, xlo] = w_out[...]

    barrier = pltpu.get_barrier_semaphore()
    peers = [strip_up, strip_down, y_up, y_down, x_near, x_far, z_up, z_down]
    for peer in peers:
        pl.semaphore_signal(barrier, inc=1, device_id=peer, device_id_type=MESH)
    pl.semaphore_wait(barrier, len(peers))

    def ring_gather(buf, half, count, sem):
        def block(zi, lo=0, n=count):
            return buf.at[zi * 2 + half, pl.ds(lo, n)]

        up = send(block(z), block(z), z_up, sem)
        down = send(block(z), block(z), z_down, sem)
        yield
        for k in (1, 2, 3):
            if k < 3:
                up.wait_recv()
                up = send(block(at_z(-k)), block(at_z(-k)), z_up, sem)
                down.wait_recv()
                down = send(block(at_z(k)), block(at_z(k)), z_down, sem)
            else:
                h = count // 2
                up.wait_recv()
                up = send(block(at_z(-3), 0, h), block(at_z(-3), 0, h), z_up, sem)
                down.wait_recv()
                down = send(block(at_z(3), h, h), block(at_z(3), h, h), z_down, sem)
            yield
        up.wait_recv()
        down.wait_recv()
        yield

    def gather_col(buf):
        sem = blocks15()
        far = []

        def rows(zi, half, first, count):
            return buf.at[zi * 2 + half, pl.ds(first, count)]

        def own():
            ring = ring_gather(buf, xhi, PIX, sem)
            near = send(rows(z, xhi, 0, n0), rows(z, xhi, 0, n0), x_far, sem)
            next(ring)
            far.append(send(rows(z, xhi, n0, n1), rows(z, xhi, n0, n1), x_far, sem))
            yield near
            for k in (1, 2, 3, 4):
                next(ring)
                for step in (-k, k) if k < 4 else (4,):
                    part = rows(at_z(step), xhi, n0, n1)
                    far.append(send(part, part, x_far, sem))
                yield

        def other(near):
            near.wait_recv()
            ring = ring_gather(buf, 1 - xhi, n0, sem)
            for k in range(5):
                next(ring)
                yield

        def rest(count):
            for copy in far[:count]:
                copy.wait_recv()
            del far[:count]

        first = own()
        second = other(next(first))
        return first, second, rest

    def gather_stats(slots):
        near = send(slots.at[0, 0], slots.at[0, 1], x_far)
        yield
        near.wait_recv()
        up = send(slots.at[0], slots.at[NZ - 1], z_up)
        down = send(slots.at[0], slots.at[1], z_down)
        yield
        for k in (1, 2, 3):
            up.wait_recv()
            up = send(slots.at[NZ - k], slots.at[NZ - k - 1], z_up)
            down.wait_recv()
            if k < 3:
                down = send(slots.at[k], slots.at[k + 1], z_down)
            yield
        up.wait_recv()
        yield

    def gather_row(buf, own):
        def block(k, yi, xi, lo=0, n=CB):
            return buf.at[k, yi, xi, pl.ds(lo, n)]
        waits = []
        sem = blocks15()

        def share(yi, xi):
            waits.append(send(block(core, yi, xi), block(core, yi, xi), sibling, sem))

        near = send(own, block(core, y, xlo), x_near, sem)
        up, down = {}, {}
        up[0] = send(own, block(core, y, xlo), y_up, sem)
        down[0] = send(own, block(core, y, xlo), y_down, sem)
        waits.append(send(own, block(core, y, xlo), sibling, sem))
        yield
        near.wait_recv()
        other = 1 - xlo
        up[1] = send(block(core, y, other), block(core, y, other), y_up, sem)
        down[1] = send(block(core, y, other), block(core, y, other), y_down, sem)
        share(y, other)
        yield
        h = CB // 2
        for i, xi in enumerate((xlo, other)):
            up[i].wait_recv()
            down[i].wait_recv()
            low, high = block(core, at_y(-1), xi, 0, h), block(core, at_y(1), xi, h, h)
            up[i] = send(low, low, y_up, sem)
            down[i] = send(high, high, y_down, sem)
            share(at_y(-1), xi)
            share(at_y(1), xi)
            yield
        for i, xi in enumerate((xlo, other)):
            up[i].wait_recv()
            down[i].wait_recv()
            share(at_y(2), xi)
        yield
        for copy in waits:
            copy.wait_recv()
        yield

    def add_into(dst, src):
        dst[...] = (dst[...].astype(F32) + src[...].astype(F32)).astype(BF16)

    def ring_scatter(buf, half, count, rm, rp, ready, sem):
        h = count // 2

        def block(zi, lo=0, n=count):
            return buf.at[zi * 2 + half, pl.ds(lo, n)]

        ready(4)
        down = send(block(at_z(-4), 0, h), rm.at[0, pl.ds(0, h)], z_down, sem)
        up = send(block(at_z(4), h, h), rp.at[0, pl.ds(0, h)], z_up, sem)
        yield
        for k in (2, 3, 4):
            dist = 5 - k
            ready(-dist)
            ready(dist)
            down.wait_recv()
            if k == 2:
                add_into(block(at_z(-dist), 0, h), rm.at[0, pl.ds(0, h)])
            else:
                add_into(block(at_z(-dist)), rm.at[k - 2])
            down = send(block(at_z(-dist)), rm.at[k - 1], z_down, sem)
            up.wait_recv()
            if k == 2:
                add_into(block(at_z(dist), h, h), rp.at[0, pl.ds(0, h)])
            else:
                add_into(block(at_z(dist)), rp.at[k - 2])
            up = send(block(at_z(dist)), rp.at[k - 1], z_up, sem)
            yield
        ready(0)
        down.wait_recv()
        up.wait_recv()
        yield

    def scatter_col(buf, rm, rp, rmo, rpo, rx, xs_, xr, total):
        sem = blocks15()
        far = {}

        def offer(step):
            zi = at_z(step)
            far[step % NZ] = send(
                buf.at[zi * 2 + 1 - xhi, pl.ds(n0, n1)], rx.at[zi], x_far, sem
            )

        def ready(step):
            zi = at_z(step)
            far[step % NZ].wait_recv()
            add_into(buf.at[zi * 2 + xhi, pl.ds(n0, n1)], rx.at[zi])

        last = []

        def other():
            half = 1 - xhi
            ring = ring_scatter(buf, half, n0, rmo, rpo, lambda step: None, sem)
            for k in range(4):
                next(ring)
                yield
            next(ring)
            xs_[...] = (
                buf[z * 2 + half, 0:n0].astype(F32) + rmo[3].astype(F32) + rpo[3].astype(F32)
            ).astype(BF16)
            last.append(send(xs_, xr, x_far, sem))
            yield

        def own():
            ring = ring_scatter(buf, xhi, PIX, rm, rp, ready, sem)
            for k in range(5):
                next(ring)
                yield
            last[0].wait_recv()
            both = buf[z * 2 + xhi].astype(F32) + rm[3].astype(F32) + rp[3].astype(F32)
            total[0:n0] = both[0:n0] + xr[...].astype(F32)
            total[n0:PIX] = both[n0:PIX]
            yield

        return offer, other(), own()

    def scatter_row(buf, rc, rm, rp, rx, xs_slot, out):
        h = CB // 2
        shared = {}
        sem = blocks15()
        for step in (2, -1, 1, 0):
            shared[step] = send(buf.at[1 - core, at_y(step)], rc.at[at_y(step)], sibling, sem)
        yield
        shared[2].wait_recv()
        add_into(buf.at[core, at_y(2)], rc.at[at_y(2)])
        down = send(
            buf.at[core, at_y(-2), :, pl.ds(0, h)], rm.at[0, :, pl.ds(0, h)], y_down, sem
        )
        up = send(buf.at[core, at_y(2), :, pl.ds(h, h)], rp.at[0, :, pl.ds(0, h)], y_up, sem)
        for step in (-1, 1, 0):
            shared[step].wait_recv()
            add_into(buf.at[core, at_y(step)], rc.at[at_y(step)])
        yield
        down.wait_recv()
        add_into(buf.at[core, at_y(-1), :, pl.ds(0, h)], rm.at[0, :, pl.ds(0, h)])
        down = send(buf.at[core, at_y(-1)], rm.at[1], y_down, sem)
        up.wait_recv()
        add_into(buf.at[core, at_y(1), :, pl.ds(h, h)], rp.at[0, :, pl.ds(0, h)])
        up = send(buf.at[core, at_y(1)], rp.at[1], y_up, sem)
        yield
        down.wait_recv()
        up.wait_recv()
        theirs = 1 - xlo
        xs_slot[0] = (
            buf[core, y, theirs].astype(F32)
            + rm[1, theirs].astype(F32)
            + rp[1, theirs].astype(F32)
        ).astype(BF16)
        near = send(xs_slot.at[0], rx.at[1], x_near, sem)
        yield
        near.wait_recv()
        out[...] = (
            buf[core, y, xlo].astype(F32)
            + rm[1, xlo].astype(F32)
            + rp[1, xlo].astype(F32)
            + rx[1].astype(F32)
        ).astype(BF16)
        yield

    def taps_sum(flipped, finish):
        def strip_row(bh, carry):
            image, line = bh // 4, bh % 4
            total = jnp.zeros((64, CB), F32)
            for i in range(KS):
                for j in range(KS):
                    tap = dwk[KS - 1 - i, pl.ds(KS - 1 - j, 1)] if flipped else dwk[i, pl.ds(j, 1)]
                    total = total + tap * pad[image, line + i, pl.ds(TAP0 + j, 64)]
            finish(bh, total)
            return carry

        lax.fori_loop(0, 8, strip_row, 0)

    def set_halo(low, high):
        pad[:, 0:3, LEFT : LEFT + 64] = jnp.where(row > 0, low[...].astype(F32), 0.0)
        pad[:, 7:10, LEFT : LEFT + 64] = jnp.where(row < 15, high[...].astype(F32), 0.0)

    lane = lax.broadcasted_iota(jnp.int32, (64, CB), 1)

    def put_sums(bh, first, second):
        tmp[pl.ds(pl.multiple_of(bh * 64, 64), 64)] = jnp.where(
            lane == 0, first, jnp.where(lane == 1, second, 0.0)
        )

    def packed_sums():
        parts = [jnp.transpose(tmp[q * 128 : (q + 1) * 128]) for q in range(4)]
        return jnp.concatenate([p[0:1] for p in parts] + [p[1:2] for p in parts], axis=0)

    def exchange_sums(slots):
        slots[col] = packed_sums()
        sem, recv = group(slots.at[0:15]), take("recv")
        for k in range(1, 16):
            send(slots.at[col], slots.at[col], col_peer(k), sem, recv)
        return pltpu.make_async_remote_copy(
            src_ref=slots.at[0:15], dst_ref=slots.at[0:15], send_sem=send_sem.at[sem],
            recv_sem=recv_sem.at[recv], device_id=col_peer(1), device_id_type=MESH,
        )

    def spread(line):
        return jnp.transpose(jnp.broadcast_to(line, (128, 128)))

    copies = [
        send(images.at[:, 1:4], halo_lo, strip_up),
        send(images.at[:, 0:3], halo_hi, strip_down),
    ]
    grads, grads2, grads_rest = gather_col(gg)
    win = gather_row(wi, w_in)
    next(win)
    wout = gather_row(wo, w_out)
    next(wout)

    for copy in copies:
        copy.wait_recv()
    set_halo(halo_lo, halo_hi)

    def after_conv(bh, total):
        part = pl.ds(pl.multiple_of(bh * 64, 64), 64)
        conv[part] = total
        mean = jnp.sum(total, axis=1, keepdims=True) * (1.0 / CB)
        dev = total - mean
        xg[col, part] = dev.astype(BF16)
        put_sums(bh, mean, jnp.sum(dev * dev, axis=1, keepdims=True))

    taps_sum(False, after_conv)
    pix, pix2, pix_rest = gather_col(xg)
    st1[0, 0, 0:8] = packed_sums()
    st1[0, 0, 8:16] = jnp.broadcast_to(gain[...], (8, CB))
    stats = gather_stats(st1)
    next(stats)

    def pair(buf, zi):
        return jnp.concatenate([buf[zi * 2], buf[zi * 2 + 1]], axis=1)

    def panel(buf, zi):
        xi, yi = zi // NY, zi % NY
        return jnp.concatenate([buf[0, yi, xi], buf[1, yi, xi]], axis=0)

    def product(acc, buf, weight, step, first):
        zi = at_z(step)
        term = jnp.dot(pair(buf, zi), panel(weight, zi), preferred_element_type=F32)
        if first:
            acc[...] = term
        else:
            acc[...] += term

    def normalise(step):
        for other in (0, 1):
            slot = (step % NZ, other)
            half = xhi if other == 0 else 1 - xhi
            place = slot[0] * 2 + other
            scale = st1[slot[0], other, 8:9]
            for q in range(4):
                part = slice(q * 128, (q + 1) * 128)
                dev = xg[at_z(step) * 2 + half, part].astype(F32)
                value = (dev + cols[q, :, place : place + 1]) * istd[part] * scale
                xs[at_z(step) * 2 + half, part] = value.astype(BF16)

    streams = dict(G=grads, g=grads2, X=pix, x=pix2, W=win, w=wout, S=stats)
    for name in GATHER_ORDER:
        next(streams[name])
    every = st1[...]
    means, devs = every[:, :, 0:4], every[:, :, 4:8]
    mean = jnp.sum(means, axis=(0, 1)) * (1.0 / 16)
    shift = means - mean[None, None]
    var = (jnp.sum(devs, axis=(0, 1)) + CB * jnp.sum(shift * shift, axis=(0, 1))) * (1.0 / C)
    inv = lax.rsqrt(var + 1e-06)
    for q in range(4):
        part = slice(q * 128, (q + 1) * 128)
        lines = [shift[o, i, q : q + 1] for o in range(NZ) for i in range(2)]
        lines += [inv[q : q + 1], mean[q : q + 1], jnp.zeros((110, 128), F32)]
        turned = jnp.transpose(jnp.concatenate(lines, axis=0))
        cols[q] = turned
        scale = jnp.broadcast_to(turned[:, 16:17], (128, CB))
        istd[part] = scale
        normed[part] = (conv[part] - turned[:, 17:18]) * scale
    grads_rest(8)
    product(gh, gg, wo, 0, True)
    for step in (1, -1, 2, -2, 3, -3, 4):
        product(gh, gg, wo, step, False)

    def gain_product(step, first):
        mine, theirs = st1[step % NZ, 0, 8:16], st1[step % NZ, 1, 8:16]
        gains = jnp.concatenate(
            [jnp.where(xhi == 0, mine, theirs), jnp.where(xhi == 0, theirs, mine)], axis=1
        )
        high = gains.astype(BF16)
        low = (gains - high.astype(F32)).astype(BF16)
        parts = jnp.concatenate([high, low], axis=0)
        term = jnp.dot(parts, panel(wi, at_z(step)), preferred_element_type=F32)
        term = term[0:8] + term[8:16]
        if first:
            gw[...] = term
        else:
            gw[...] += term

    for step in (0, 1, -1, 2, -2, 3, -3, 4):
        gain_product(step, step == 0)
    for count, steps in ((1, (0,)), (2, (1, -1)), (2, (2, -2)), (3, (3, -3, 4))):
        pix_rest(count)
        for step in steps:
            normalise(step)
            product(hp, xs, wi, step, step == 0)

    def activate(i, carry):
        part = pl.ds(pl.multiple_of(i * 64, 64), 64)
        v = hp[part]
        cdf = 0.5 * (1.0 + lax.erf(v * 0.7071067811865476))
        slope = cdf + v * jnp.exp(-0.5 * v * v) * 0.3989422804014327
        hid[part] = (v * cdf).astype(BF16)
        grad = (gh[part] * slope).astype(BF16)
        gpre[part] = grad
        grad = grad.astype(F32)
        put_sums(
            i,
            jnp.sum(grad * gw[0:1], axis=1, keepdims=True),
            jnp.sum(grad * v, axis=1, keepdims=True),
        )
        return carry

    lax.fori_loop(0, 8, activate, 0)

    def to_channels(dst, act, weight, step):
        zi = at_z(step)
        term = lax.dot_general(
            act[...], panel(weight, zi), CONTRACT_LAST, preferred_element_type=F32
        ).astype(BF16)
        dst[zi * 2] = term[:, 0:CB]
        dst[zi * 2 + 1] = term[:, CB : 2 * CB]

    def weight_grad(dst, buf, act):
        def one(zi, carry):
            xi, yi = zi // NY, zi % NY
            term = lax.dot_general(
                pair(buf, zi), act[...], CONTRACT_FIRST, preferred_element_type=F32
            ).astype(BF16)
            dst[0, yi, xi] = term[0:CB]
            dst[1, yi, xi] = term[CB : 2 * CB]
            return carry

        lax.fori_loop(0, NZ, one, 0)

    steps = (4, -3, 3, -2, 2, -1, 1, 0)
    offer_b, back2, back = scatter_col(bk, bk_m, bk_p, bk_mo, bk_po, bk_x, bk_xs, bk_xr, gs)
    offer_c, branch2, branch = scatter_col(
        cb, cb_m, cb_p, cb_mo, cb_po, cb_x, cb_xs, cb_xr, hp.at[:, 0:CB]
    )
    for step in steps:
        to_channels(bk, gpre, wi, step)
        offer_b(step)
        if step == 4:
            next(back2)
    totals = exchange_sums(st2)
    streams = dict(
        b=back2, B=back, c=branch2, C=branch,
        M=scatter_row(g2, g2_c, g2_m, g2_p, g2_r, g2_r, gp_out),
        N=scatter_row(g1, g1_c, g1_m, g1_p, g1_r, g1_r, gp_in),
    )

    def contrib():
        for step in steps:
            to_channels(cb, hid, wo, step)
            offer_c(step)
            if step == 4:
                next(branch2)

    def run(order):
        for name in order:
            if name == "k":
                contrib()
            elif name == "m":
                weight_grad(g2, gg, hid)
            elif name == "n":
                weight_grad(g1, xs, gpre)
            else:
                next(streams[name])

    run(BACK_ORDER)

    totals.wait_recv()
    total = jnp.sum(st2[...], axis=0) * (1.0 / C)
    for q in range(4):
        part = slice(q * 128, (q + 1) * 128)
        value = istd[part] * (
            gs[part] * gain[...] - spread(total[q : q + 1]) - normed[part] * spread(total[4 + q : 5 + q])
        )
        image, line = q // 2, 2 * (q % 2)
        value = value.reshape(2, 64, CB)
        pad[image, 3 + line : 5 + line, LEFT : LEFT + 64] = value
        value = value.astype(BF16)
        if line == 0:
            edge_hi[image, 0:2] = value
            edge_lo[image, 0:1] = value[1:2]
        else:
            edge_hi[image, 2:3] = value[0:1]
            edge_lo[image, 1:3] = value
    copies = [send(edge_lo, ghalo_lo, strip_up), send(edge_hi, ghalo_hi, strip_down)]
    run(HALO_ORDER)
    for copy in copies:
        copy.wait_recv()
    set_halo(ghalo_lo, ghalo_hi)

    def after_transposed(bh, total):
        part = pl.ds(pl.multiple_of(bh * 64, 64), 64)
        grad_images[bh // 4, bh % 4] = (cot[part].astype(F32) + total).astype(BF16)

    taps_sum(True, after_transposed)

    run(LAST_ORDER)
    branch_sum = hp.at[:, 0:CB]
    for q in range(8):
        part = slice(q * 64, (q + 1) * 64)
        image, line = q // 4, q % 4
        block_out[image, line] = (
            images[image, line].astype(F32) + lscale[...] * branch_sum[part]
        ).astype(BF16)
    for sem, whole in sends:
        pltpu.make_async_remote_copy(
            src_ref=whole, dst_ref=whole, send_sem=send_sem.at[sem], recv_sem=recv_sem.at[0],
            device_id=z_up, device_id_type=MESH,
        ).wait_send()
    assert counts["recv"] <= N_RECV and counts["send"] <= N_SEND, counts
    for name, stream in streams.items():
        assert next(stream, None) is None, name


def on_device(images, dw_kernel, norm_gain, proj_in, proj_out, layer_scale, cotangent):
    n0 = 256
    n1 = PIX - n0
    strip = images.shape
    vmem = pltpu.VMEM
    col_blocks = vmem((2 * NZ, PIX, CB), BF16)
    row_blocks = vmem((2, NY, 2, CB, HB), BF16)
    scratch = (
        [vmem((2, 10, 64 + 2 * LEFT, CB), F32)]
        + [vmem((2, 3, 64, CB), BF16)] * 6
        + [vmem((PIX, CB), F32)] * 4
        + [vmem((NZ, 2, 16, CB), F32), vmem((16, 8, CB), F32), vmem((4, 128, 128), F32)]
        + [col_blocks] * 3
        + [row_blocks] * 2
        + [vmem((PIX, HB), F32)] * 2
        + [vmem((PIX, HB), BF16)] * 2
        + [vmem((8, HB), F32)]
        + [col_blocks] * 2
        + [vmem((4, PIX, CB), BF16)] * 4
        + [vmem((4, n0, CB), BF16)] * 4
        + [vmem((NZ, n1, CB), BF16)] * 2
        + [vmem((n0, CB), BF16)] * 4
        + [vmem((PIX, CB), F32)]
        + [row_blocks] * 2
        + [vmem((NY, 2, CB, HB), BF16)] * 2
        + [vmem((2, 2, CB, HB), BF16)] * 4
        + [vmem((2, CB, HB), BF16)] * 2
        + [pltpu.SemaphoreType.DMA((N_SEND,)), pltpu.SemaphoreType.DMA((N_RECV,))]
    )
    block = pl.BlockSpec(memory_space=pltpu.VMEM)
    return pl.pallas_call(
        functools.partial(kernel, n0),
        out_shape=(
            jax.ShapeDtypeStruct(strip, BF16),
            jax.ShapeDtypeStruct(strip, BF16),
            jax.ShapeDtypeStruct(proj_in.shape, BF16),
            jax.ShapeDtypeStruct(proj_out.shape, BF16),
        ),
        in_specs=[block] * 7,
        out_specs=(block,) * 4,
        scratch_shapes=scratch,
        compiler_params=pltpu.CompilerParams(
            collective_id=0, has_side_effects=True, vmem_limit_bytes=56 << 20
        ),
    )(
        images,
        dw_kernel,
        norm_gain.reshape(1, CB),
        proj_in,
        proj_out,
        layer_scale.reshape(1, CB),
        cotangent.reshape(PIX, CB),
    )


def solution(mesh):
    placed = (
        P(None, "row", None, "col"),
        P(None, None, "col"),
        P("col"),
        P("row", "col"),
        P("row", "col"),
        P("col"),
        P(None, "row", None, "col"),
    )
    return jax.shard_map(
        on_device,
        mesh=mesh,
        in_specs=placed,
        out_specs=(
            P(None, "row", None, "col"),
            P(None, "row", None, "col"),
            P("row", "col"),
            P("row", "col"),
        ),
        check_vma=False,
    )
```

```python
import functools

import jax
import jax.numpy as jnp
from jax import lax
from jax.experimental import pallas as pl
from jax.experimental.pallas import tpu as pltpu
from jax.sharding import PartitionSpec as P

MESH = pl.DeviceIdType.MESH
F32, BF16 = jnp.float32, jnp.bfloat16
C = 2048
KS = 7
NZ, NY = 8, 4
CB = 128
HB = 512
PIX = 512
LEFT = 8
TAP0 = LEFT - KS // 2
N_SEND, N_RECV = 21, 165
PRE_ORDER = ""
MID_ORDER = ""
GATHER_ORDER = "gGWwxXSgGWwSxXgGWwSxXgGWwSxXgWwpSq012x34"
BACK_ORDER = "mMBnNbBkMbBcCNbBcCMsbBNB"
HALO_ORDER = "cCMN"
LAST_ORDER = "cCMNCC"
CONTRACT_LAST = (((1,), (1,)), ((), ()))
CONTRACT_FIRST = (((0,), (0,)), ((), ()))


def kernel(
    n0,
    images, dwk, gain, w_in, w_out, lscale, cot,
    block_out, grad_images, gp_in, gp_out,
    pad, halo_lo, halo_hi, ghalo_lo, ghalo_hi, edge_lo, edge_hi,
    conv, normed, istd, tmp, st1, st2,
    cols, xg, xs, gg, wi, wo, hp, gh, hid, gpre,
    less, gw, cb, bk, cb_m, cb_p, bk_m, bk_p, cb_mo, cb_po, bk_mo, bk_po,
    cb_x, bk_x, cb_xs, bk_xs, cb_xr, bk_xr, gs,
    g1, g2, g1_c, g2_c, g1_m, g1_p, g2_m, g2_p, g1_r, g2_r,
    send_sem, recv_sem,
):
    n1 = PIX - n0
    row, col = lax.axis_index("row"), lax.axis_index("col")
    xlo, y, core = row // 8, (row // 2) % NY, row % 2
    z, xhi = col // 2, col % 2

    def at_z(step):
        return (z + step + NZ) % NZ

    def at_y(step):
        return (y + step + NY) % NY

    z_up = {"row": row, "col": at_z(1) * 2 + xhi}
    z_down = {"row": row, "col": at_z(-1) * 2 + xhi}
    x_far = {"row": row, "col": z * 2 + (1 - xhi)}
    y_up = {"row": xlo * 8 + at_y(1) * 2 + core, "col": col}
    y_down = {"row": xlo * 8 + at_y(-1) * 2 + core, "col": col}
    x_near = {"row": (1 - xlo) * 8 + y * 2 + core, "col": col}
    sibling = {"row": xlo * 8 + y * 2 + (1 - core), "col": col}
    strip_up = {"row": (row + 1) % 16, "col": col}
    strip_down = {"row": (row + 15) % 16, "col": col}

    def col_peer(step):
        return {"row": row, "col": (col + step) % 16}

    counts = {"recv": 0, "send": 0}

    def take(kind):
        counts[kind] += 1
        return counts[kind] - 1

    sends = []

    def group(whole):
        sends.append((take("send"), whole))
        return sends[-1][0]

    def send(src, dst, where, sem=None, recv=None):
        if sem is None:
            sem = group(src)
        copy = pltpu.make_async_remote_copy(
            src_ref=src, dst_ref=dst, send_sem=send_sem.at[sem],
            recv_sem=recv_sem.at[take("recv") if recv is None else recv],
            device_id=where, device_id_type=MESH,
        )
        copy.start()
        return copy

    def blocks15():
        return group(xg.at[0:15])

    barrier = pltpu.get_barrier_semaphore()
    peers = [strip_up, strip_down, y_up, y_down, x_near, x_far, z_up, z_down]
    for peer in peers:
        pl.semaphore_signal(barrier, inc=1, device_id=peer, device_id_type=MESH)
    zero_edge = jnp.zeros((2, 10, LEFT, CB), F32)
    pad[:, :, 0:LEFT] = zero_edge
    pad[:, :, LEFT + 64 : 2 * LEFT + 64] = zero_edge
    pad[:, 3:7, LEFT : LEFT + 64] = images[...].astype(F32)
    for q in range(4):
        part = slice(q * 128, (q + 1) * 128)
        gg[col, part] = (cot[part].astype(F32) * lscale[...]).astype(BF16)
    wi[core, y, xlo] = w_in[...]
    wo[core, y, xlo] = w_out[...]
    pl.semaphore_wait(barrier, len(peers))

    def ring_gather(buf, half, count, sem):
        def block(zi, lo=0, n=count):
            return buf.at[zi * 2 + half, pl.ds(lo, n)]

        up = send(block(z), block(z), z_up, sem)
        down = send(block(z), block(z), z_down, sem)
        yield
        for k in (1, 2, 3):
            if k < 3:
                up.wait_recv()
                up = send(block(at_z(-k)), block(at_z(-k)), z_up, sem)
                down.wait_recv()
                down = send(block(at_z(k)), block(at_z(k)), z_down, sem)
            else:
                h = count // 2
                up.wait_recv()
                up = send(block(at_z(-3), 0, h), block(at_z(-3), 0, h), z_up, sem)
                down.wait_recv()
                down = send(block(at_z(3), h, h), block(at_z(3), h, h), z_down, sem)
            yield
        up.wait_recv()
        down.wait_recv()
        yield

    def gather_col(buf):
        sem = blocks15()
        far = []

        def rows(zi, half, first, count):
            return buf.at[zi * 2 + half, pl.ds(first, count)]

        def own():
            ring = ring_gather(buf, xhi, PIX, sem)
            near = send(rows(z, xhi, 0, n0), rows(z, xhi, 0, n0), x_far, sem)
            next(ring)
            far.append(send(rows(z, xhi, n0, n1), rows(z, xhi, n0, n1), x_far, sem))
            yield near
            for k in (1, 2, 3, 4):
                next(ring)
                for step in (-k, k) if k < 4 else (4,):
                    part = rows(at_z(step), xhi, n0, n1)
                    far.append(send(part, part, x_far, sem))
                yield

        def other(near):
            near.wait_recv()
            ring = ring_gather(buf, 1 - xhi, n0, sem)
            for k in range(5):
                next(ring)
                yield

        def rest(count):
            for copy in far[:count]:
                copy.wait_recv()
            del far[:count]

        first = own()
        second = other(next(first))
        return first, second, rest

    def gather_stats(slots):
        near = send(slots.at[0, 0], slots.at[0, 1], x_far)
        yield
        near.wait_recv()
        up = send(slots.at[0], slots.at[NZ - 1], z_up)
        down = send(slots.at[0], slots.at[1], z_down)
        yield
        for k in (1, 2, 3):
            up.wait_recv()
            up = send(slots.at[NZ - k], slots.at[NZ - k - 1], z_up)
            down.wait_recv()
            if k < 3:
                down = send(slots.at[k], slots.at[k + 1], z_down)
            yield
        up.wait_recv()
        yield

    def gather_row(buf, own):
        def block(k, yi, xi, lo=0, n=CB):
            return buf.at[k, yi, xi, pl.ds(lo, n)]
        waits = []
        sem = blocks15()

        def share(yi, xi):
            waits.append(send(block(core, yi, xi), block(core, yi, xi), sibling, sem))

        near = send(own, block(core, y, xlo), x_near, sem)
        up, down = {}, {}
        up[0] = send(own, block(core, y, xlo), y_up, sem)
        down[0] = send(own, block(core, y, xlo), y_down, sem)
        waits.append(send(own, block(core, y, xlo), sibling, sem))
        yield
        near.wait_recv()
        other = 1 - xlo
        up[1] = send(block(core, y, other), block(core, y, other), y_up, sem)
        down[1] = send(block(core, y, other), block(core, y, other), y_down, sem)
        share(y, other)
        yield
        h = CB // 2
        for i, xi in enumerate((xlo, other)):
            up[i].wait_recv()
            down[i].wait_recv()
            low, high = block(core, at_y(-1), xi, 0, h), block(core, at_y(1), xi, h, h)
            up[i] = send(low, low, y_up, sem)
            down[i] = send(high, high, y_down, sem)
            share(at_y(-1), xi)
            share(at_y(1), xi)
            yield
        for i, xi in enumerate((xlo, other)):
            up[i].wait_recv()
            down[i].wait_recv()
            share(at_y(2), xi)
        yield
        for copy in waits:
            copy.wait_recv()
        yield

    def add_into(dst, src):
        dst[...] = (dst[...].astype(F32) + src[...].astype(F32)).astype(BF16)

    def ring_scatter(buf, half, count, rm, rp, ready, sem):
        h = count // 2

        def block(zi, lo=0, n=count):
            return buf.at[zi * 2 + half, pl.ds(lo, n)]

        ready(4)
        down = send(block(at_z(-4), 0, h), rm.at[0, pl.ds(0, h)], z_down, sem)
        up = send(block(at_z(4), h, h), rp.at[0, pl.ds(0, h)], z_up, sem)
        yield
        for k in (2, 3, 4):
            dist = 5 - k
            ready(-dist)
            ready(dist)
            down.wait_recv()
            if k == 2:
                add_into(block(at_z(-dist), 0, h), rm.at[0, pl.ds(0, h)])
            else:
                add_into(block(at_z(-dist)), rm.at[k - 2])
            down = send(block(at_z(-dist)), rm.at[k - 1], z_down, sem)
            up.wait_recv()
            if k == 2:
                add_into(block(at_z(dist), h, h), rp.at[0, pl.ds(0, h)])
            else:
                add_into(block(at_z(dist)), rp.at[k - 2])
            up = send(block(at_z(dist)), rp.at[k - 1], z_up, sem)
            yield
        ready(0)
        down.wait_recv()
        up.wait_recv()
        yield

    def scatter_col(buf, rm, rp, rmo, rpo, rx, xs_, xr, total):
        sem = blocks15()
        far = {}

        def offer(step):
            zi = at_z(step)
            far[step % NZ] = send(
                buf.at[zi * 2 + 1 - xhi, pl.ds(n0, n1)], rx.at[zi], x_far, sem
            )

        def ready(step):
            zi = at_z(step)
            far[step % NZ].wait_recv()
            add_into(buf.at[zi * 2 + xhi, pl.ds(n0, n1)], rx.at[zi])

        last = []

        def other():
            half = 1 - xhi
            ring = ring_scatter(buf, half, n0, rmo, rpo, lambda step: None, sem)
            for k in range(4):
                next(ring)
                yield
            next(ring)
            xs_[...] = (
                buf[z * 2 + half, 0:n0].astype(F32) + rmo[3].astype(F32) + rpo[3].astype(F32)
            ).astype(BF16)
            last.append(send(xs_, xr, x_far, sem))
            yield

        def own():
            ring = ring_scatter(buf, xhi, PIX, rm, rp, ready, sem)
            for k in range(5):
                next(ring)
                yield
            last[0].wait_recv()
            both = buf[z * 2 + xhi].astype(F32) + rm[3].astype(F32) + rp[3].astype(F32)
            total[0:n0] = both[0:n0] + xr[...].astype(F32)
            total[n0:PIX] = both[n0:PIX]
            yield

        return offer, other(), own()

    def scatter_row(buf, rc, rm, rp, rx, xs_slot, out):
        h = CB // 2
        shared = {}
        sem = blocks15()
        for step in (2, -1, 1, 0):
            shared[step] = send(buf.at[1 - core, at_y(step)], rc.at[at_y(step)], sibling, sem)
        yield
        shared[2].wait_recv()
        add_into(buf.at[core, at_y(2)], rc.at[at_y(2)])
        down = send(
            buf.at[core, at_y(-2), :, pl.ds(0, h)], rm.at[0, :, pl.ds(0, h)], y_down, sem
        )
        up = send(buf.at[core, at_y(2), :, pl.ds(h, h)], rp.at[0, :, pl.ds(0, h)], y_up, sem)
        for step in (-1, 1, 0):
            shared[step].wait_recv()
            add_into(buf.at[core, at_y(step)], rc.at[at_y(step)])
        yield
        down.wait_recv()
        add_into(buf.at[core, at_y(-1), :, pl.ds(0, h)], rm.at[0, :, pl.ds(0, h)])
        down = send(buf.at[core, at_y(-1)], rm.at[1], y_down, sem)
        up.wait_recv()
        add_into(buf.at[core, at_y(1), :, pl.ds(h, h)], rp.at[0, :, pl.ds(0, h)])
        up = send(buf.at[core, at_y(1)], rp.at[1], y_up, sem)
        yield
        down.wait_recv()
        up.wait_recv()
        theirs = 1 - xlo
        xs_slot[0] = (
            buf[core, y, theirs].astype(F32)
            + rm[1, theirs].astype(F32)
            + rp[1, theirs].astype(F32)
        ).astype(BF16)
        near = send(xs_slot.at[0], rx.at[1], x_near, sem)
        yield
        near.wait_recv()
        out[...] = (
            buf[core, y, xlo].astype(F32)
            + rm[1, xlo].astype(F32)
            + rp[1, xlo].astype(F32)
            + rx[1].astype(F32)
        ).astype(BF16)
        yield

    def taps_sum(flipped, finish):
        def strip_row(bh, carry):
            image, line = bh // 4, bh % 4
            total = jnp.zeros((64, CB), F32)
            for i in range(KS):
                for j in range(KS):
                    tap = dwk[KS - 1 - i, pl.ds(KS - 1 - j, 1)] if flipped else dwk[i, pl.ds(j, 1)]
                    total = total + tap * pad[image, line + i, pl.ds(TAP0 + j, 64)]
            finish(bh, total)
            return carry

        lax.fori_loop(0, 8, strip_row, 0)

    def set_halo(low, high):
        pad[:, 0:3, LEFT : LEFT + 64] = jnp.where(row > 0, low[...].astype(F32), 0.0)
        pad[:, 7:10, LEFT : LEFT + 64] = jnp.where(row < 15, high[...].astype(F32), 0.0)

    lane = lax.broadcasted_iota(jnp.int32, (64, CB), 1)

    def put_sums(bh, first, second):
        tmp[pl.ds(pl.multiple_of(bh * 64, 64), 64)] = jnp.where(
            lane == 0, first, jnp.where(lane == 1, second, 0.0)
        )

    def packed_sums():
        parts = [jnp.transpose(tmp[q * 128 : (q + 1) * 128]) for q in range(4)]
        return jnp.concatenate([p[0:1] for p in parts] + [p[1:2] for p in parts], axis=0)

    def exchange_sums(slots):
        slots[col] = packed_sums()
        sem, recv = group(slots.at[0:15]), take("recv")
        for k in range(1, 16):
            send(slots.at[col], slots.at[col], col_peer(k), sem, recv)
        return pltpu.make_async_remote_copy(
            src_ref=slots.at[0:15], dst_ref=slots.at[0:15], send_sem=send_sem.at[sem],
            recv_sem=recv_sem.at[recv], device_id=col_peer(1), device_id_type=MESH,
        )

    def spread(line):
        return jnp.transpose(jnp.broadcast_to(line, (128, 128)))

    copies = [
        send(images.at[:, 1:4], halo_lo, strip_up),
        send(images.at[:, 0:3], halo_hi, strip_down),
    ]
    grads, grads2, grads_rest = gather_col(gg)
    win = gather_row(wi, w_in)
    next(win)
    wout = gather_row(wo, w_out)
    next(wout)

    streams = dict(G=grads, g=grads2, W=win, w=wout)

    def run(order):
        for name in order:
            next(streams[name])

    run(PRE_ORDER)

    for copy in copies:
        copy.wait_recv()
    set_halo(halo_lo, halo_hi)

    def after_conv(bh, total):
        part = pl.ds(pl.multiple_of(bh * 64, 64), 64)
        conv[part] = total
        mean = jnp.sum(total, axis=1, keepdims=True) * (1.0 / CB)
        dev = total - mean
        xg[col, part] = dev.astype(BF16)
        put_sums(bh, mean, jnp.sum(dev * dev, axis=1, keepdims=True))

    taps_sum(False, after_conv)
    run(MID_ORDER)
    pix, pix2, pix_rest = gather_col(xg)
    st1[0, 0, 0:8] = packed_sums()
    st1[0, 0, 8:16] = jnp.broadcast_to(gain[...], (8, CB))
    stats = gather_stats(st1)
    next(stats)

    def pair(buf, zi):
        return jnp.concatenate([buf[zi * 2], buf[zi * 2 + 1]], axis=1)

    def panel(buf, zi):
        xi, yi = zi // NY, zi % NY
        return jnp.concatenate([buf[0, yi, xi], buf[1, yi, xi]], axis=0)

    def product(acc, buf, weight, step, first):
        zi = at_z(step)
        term = jnp.dot(pair(buf, zi), panel(weight, zi), preferred_element_type=F32)
        if first:
            acc[...] = term
        else:
            acc[...] += term

    def statistics():
        every = st1[...]
        means, devs = every[:, :, 0:4], every[:, :, 4:8]
        mean = jnp.sum(means, axis=(0, 1)) * (1.0 / 16)
        shift = means - mean[None, None]
        var = (jnp.sum(devs, axis=(0, 1)) + CB * jnp.sum(shift * shift, axis=(0, 1))) * (1.0 / C)
        inv = lax.rsqrt(var + 1e-06)
        for q in range(4):
            part = slice(q * 128, (q + 1) * 128)
            lines = [shift[o, i, q : q + 1] for o in range(NZ) for i in range(2)]
            lines += [inv[q : q + 1], mean[q : q + 1], jnp.zeros((110, 128), F32)]
            turned = jnp.transpose(jnp.concatenate(lines, axis=0))
            cols[q] = turned
            scale = jnp.broadcast_to(turned[:, 16:17], (128, CB))
            istd[part] = scale
            normed[part] = (conv[part] - turned[:, 17:18]) * scale

    def gain_product(step, first):
        mine, theirs = st1[step % NZ, 0, 8:16], st1[step % NZ, 1, 8:16]
        gains = jnp.concatenate(
            [jnp.where(xhi == 0, mine, theirs), jnp.where(xhi == 0, theirs, mine)], axis=1
        )
        high = gains.astype(BF16)
        low = (gains - high.astype(F32)).astype(BF16)
        parts = jnp.concatenate([high, low], axis=0)
        term = jnp.dot(parts, panel(wi, at_z(step)), preferred_element_type=F32)
        term = term[0:8] + term[8:16]
        if first:
            gw[...] = term
        else:
            gw[...] += term

    def normalise(step):
        for other in (0, 1):
            slot = (step % NZ, other)
            half = xhi if other == 0 else 1 - xhi
            place = slot[0] * 2 + other
            scale = st1[slot[0], other, 8:9]
            for q in range(4):
                part = slice(q * 128, (q + 1) * 128)
                dev = xg[at_z(step) * 2 + half, part].astype(F32)
                value = (dev + cols[q, :, place : place + 1]) * istd[part] * scale
                xs[at_z(step) * 2 + half, part] = value.astype(BF16)

    around = (0, 1, -1, 2, -2, 3, -3, 4)

    def grad_hidden():
        grads_rest(8)
        for step in around:
            product(gh, gg, wo, step, step == 0)

    def finish_stats():
        statistics()
        for step in around:
            gain_product(step, step == 0)

    def pre_activation(distance):
        steps = around[max(0, 2 * distance - 1) : 2 * distance + 1]
        pix_rest(len(steps))
        for step in steps:
            normalise(step)
            product(hp, xs, wi, step, step == 0)

    def run(order):
        work = {"p": grad_hidden, "q": finish_stats}
        for name in order:
            if name in "01234":
                pre_activation(int(name))
            elif name in work:
                work[name]()
            else:
                next(streams[name])

    streams.update(X=pix, x=pix2, S=stats)
    run(GATHER_ORDER)

    def activate(i, carry):
        part = pl.ds(pl.multiple_of(i * 64, 64), 64)
        v = hp[part]
        cdf = 0.5 * (1.0 + lax.erf(v * 0.7071067811865476))
        slope = cdf + v * jnp.exp(-0.5 * v * v) * 0.3989422804014327
        hid[part] = (v * cdf).astype(BF16)
        grad = (gh[part] * slope).astype(BF16)
        gpre[part] = grad
        grad = grad.astype(F32)
        put_sums(
            i,
            jnp.sum(grad * gw[0:1], axis=1, keepdims=True),
            jnp.sum(grad * v, axis=1, keepdims=True),
        )
        return carry

    lax.fori_loop(0, 8, activate, 0)

    def to_channels(dst, act, weight, step):
        zi = at_z(step)
        term = lax.dot_general(
            act[...], panel(weight, zi), CONTRACT_LAST, preferred_element_type=F32
        ).astype(BF16)
        dst[zi * 2] = term[:, 0:CB]
        dst[zi * 2 + 1] = term[:, CB : 2 * CB]

    def weight_grad(dst, buf, act):
        def one(zi, carry):
            xi, yi = zi // NY, zi % NY
            term = lax.dot_general(
                pair(buf, zi), act[...], CONTRACT_FIRST, preferred_element_type=F32
            ).astype(BF16)
            dst[0, yi, xi] = term[0:CB]
            dst[1, yi, xi] = term[CB : 2 * CB]
            return carry

        lax.fori_loop(0, NZ, one, 0)

    steps = (4, -3, 3, -2, 2, -1, 1, 0)
    offer_b, back2, back = scatter_col(bk, bk_m, bk_p, bk_mo, bk_po, bk_x, bk_xs, bk_xr, gs)
    offer_c, branch2, branch = scatter_col(
        cb, cb_m, cb_p, cb_mo, cb_po, cb_x, cb_xs, cb_xr, hp.at[:, 0:CB]
    )
    for step in steps:
        to_channels(bk, gpre, wi, step)
        offer_b(step)
        if step == 4:
            next(back2)
    totals = exchange_sums(st2)
    streams = dict(
        b=back2, B=back, c=branch2, C=branch,
        M=scatter_row(g2, g2_c, g2_m, g2_p, g2_r, g2_r, gp_out),
        N=scatter_row(g1, g1_c, g1_m, g1_p, g1_r, g1_r, gp_in),
    )

    def contrib():
        for step in steps:
            to_channels(cb, hid, wo, step)
            offer_c(step)
            if step == 4:
                next(branch2)

    def run(order):
        for name in order:
            if name == "k":
                contrib()
            elif name == "m":
                weight_grad(g2, gg, hid)
            elif name == "n":
                weight_grad(g1, xs, gpre)
            elif name == "s":
                norm_terms()
            else:
                next(streams[name])

    def norm_terms():
        totals.wait_recv()
        total = jnp.sum(st2[...], axis=0) * (1.0 / C)
        for q in range(4):
            part = slice(q * 128, (q + 1) * 128)
            less[part] = istd[part] * (
                spread(total[q : q + 1]) + normed[part] * spread(total[4 + q : 5 + q])
            )

    run(BACK_ORDER)

    for q in range(4):
        part = slice(q * 128, (q + 1) * 128)
        value = istd[part] * (gs[part] * gain[...]) - less[part]
        image, line = q // 2, 2 * (q % 2)
        value = value.reshape(2, 64, CB)
        pad[image, 3 + line : 5 + line, LEFT : LEFT + 64] = value
        value = value.astype(BF16)
        if line == 0:
            edge_hi[image, 0:2] = value
            edge_lo[image, 0:1] = value[1:2]
        else:
            edge_hi[image, 2:3] = value[0:1]
            edge_lo[image, 1:3] = value
    copies = [send(edge_lo, ghalo_lo, strip_up), send(edge_hi, ghalo_hi, strip_down)]
    run(HALO_ORDER)
    for copy in copies:
        copy.wait_recv()
    set_halo(ghalo_lo, ghalo_hi)

    def after_transposed(bh, total):
        part = pl.ds(pl.multiple_of(bh * 64, 64), 64)
        grad_images[bh // 4, bh % 4] = (cot[part].astype(F32) + total).astype(BF16)

    taps_sum(True, after_transposed)

    run(LAST_ORDER)
    branch_sum = hp.at[:, 0:CB]
    for q in range(8):
        part = slice(q * 64, (q + 1) * 64)
        image, line = q // 4, q % 4
        block_out[image, line] = (
            images[image, line].astype(F32) + lscale[...] * branch_sum[part]
        ).astype(BF16)
    for sem, whole in sends:
        pltpu.make_async_remote_copy(
            src_ref=whole, dst_ref=whole, send_sem=send_sem.at[sem], recv_sem=recv_sem.at[0],
            device_id=z_up, device_id_type=MESH,
        ).wait_send()
    assert counts["recv"] <= N_RECV and counts["send"] <= N_SEND, counts
    for name, stream in streams.items():
        assert next(stream, None) is None, name


def hand_out(*refs):
    for i in range(4):
        refs[4 + i][...] = refs[i][...]


def on_device(images, dw_kernel, norm_gain, proj_in, proj_out, layer_scale, cotangent):
    n0 = 256
    n1 = PIX - n0
    strip = images.shape
    vmem = pltpu.VMEM
    col_blocks = vmem((2 * NZ, PIX, CB), BF16)
    row_blocks = vmem((2, NY, 2, CB, HB), BF16)
    scratch = (
        [vmem((2, 10, 64 + 2 * LEFT, CB), F32)]
        + [vmem((2, 3, 64, CB), BF16)] * 6
        + [vmem((PIX, CB), F32)] * 4
        + [vmem((NZ, 2, 16, CB), F32), vmem((16, 8, CB), F32), vmem((4, 128, 128), F32)]
        + [col_blocks] * 3
        + [row_blocks] * 2
        + [vmem((PIX, HB), F32)] * 2
        + [vmem((PIX, HB), BF16)] * 2
        + [vmem((PIX, CB), F32), vmem((8, HB), F32)]
        + [col_blocks] * 2
        + [vmem((4, PIX, CB), BF16)] * 4
        + [vmem((4, n0, CB), BF16)] * 4
        + [vmem((NZ, n1, CB), BF16)] * 2
        + [vmem((n0, CB), BF16)] * 4
        + [vmem((PIX, CB), F32)]
        + [row_blocks] * 2
        + [vmem((NY, 2, CB, HB), BF16)] * 2
        + [vmem((2, 2, CB, HB), BF16)] * 4
        + [vmem((2, CB, HB), BF16)] * 2
        + [pltpu.SemaphoreType.DMA((N_SEND,)), pltpu.SemaphoreType.DMA((N_RECV,))]
    )
    block = pl.BlockSpec(memory_space=pltpu.VMEM)
    outs = pl.pallas_call(
        functools.partial(kernel, n0),
        out_shape=(
            jax.ShapeDtypeStruct(strip, BF16),
            jax.ShapeDtypeStruct(strip, BF16),
            jax.ShapeDtypeStruct(proj_in.shape, BF16),
            jax.ShapeDtypeStruct(proj_out.shape, BF16),
        ),
        in_specs=[block] * 7,
        out_specs=(block,) * 4,
        scratch_shapes=scratch,
        compiler_params=pltpu.CompilerParams(
            collective_id=0, has_side_effects=True, vmem_limit_bytes=56 << 20
        ),
    )(
        images,
        dw_kernel,
        norm_gain.reshape(1, CB),
        proj_in,
        proj_out,
        layer_scale.reshape(1, CB),
        cotangent.reshape(PIX, CB),
    )
    return pl.pallas_call(
        hand_out,
        out_shape=tuple(jax.ShapeDtypeStruct(out.shape, out.dtype) for out in outs),
        in_specs=[block] * 4,
        out_specs=(block,) * 4,
    )(*outs)


def solution(mesh):
    placed = (
        P(None, "row", None, "col"),
        P(None, None, "col"),
        P("col"),
        P("row", "col"),
        P("row", "col"),
        P("col"),
        P(None, "row", None, "col"),
    )
    return jax.shard_map(
        on_device,
        mesh=mesh,
        in_specs=placed,
        out_specs=(
            P(None, "row", None, "col"),
            P(None, "row", None, "col"),
            P("row", "col"),
            P("row", "col"),
        ),
        check_vma=False,
    )
```

```python
import functools

import jax
import jax.numpy as jnp
from jax import lax
from jax.experimental import pallas as pl
from jax.experimental.pallas import tpu as pltpu
from jax.sharding import PartitionSpec as P

MESH = pl.DeviceIdType.MESH
F32, BF16 = jnp.float32, jnp.bfloat16
C = 2048
KS = 7
NZ, NY = 8, 4
CB = 128
HB = 512
PIX = 512
LEFT = 8
TAP0 = LEFT - KS // 2
N_SEND, N_RECV = 21, 165
PRE_ORDER = ""
MID_ORDER = ""
GATHER_ORDER = "gGxXSgGSxXWwgGWwSxXWwgGWwSxXgWwpSq012x34"
BACK_ORDER = "mMBnNbBkMbBcCNbBcCMsbBNB"
HALO_ORDER = "cCMN"
LAST_ORDER = "cCMNCC"
CONTRACT_LAST = (((1,), (1,)), ((), ()))
CONTRACT_FIRST = (((0,), (0,)), ((), ()))


def kernel(
    n0,
    images, dwk, gain, w_in, w_out, lscale, cot,
    block_out, grad_images, gp_in, gp_out,
    pad, halo_lo, halo_hi, ghalo_lo, ghalo_hi, edge_lo, edge_hi,
    conv, normed, istd, tmp, st1, st2,
    cols, xg, xs, gg, wi, wo, hp, gh, hid, gpre,
    less, gw, cb, bk, cb_m, cb_p, bk_m, bk_p, cb_mo, cb_po, bk_mo, bk_po,
    cb_x, bk_x, cb_xs, bk_xs, cb_xr, bk_xr, gs,
    g1, g2, g1_c, g2_c, g1_m, g1_p, g2_m, g2_p, g1_r, g2_r,
    send_sem, recv_sem,
):
    n1 = PIX - n0
    row, col = lax.axis_index("row"), lax.axis_index("col")
    xlo, y, core = row // 8, (row // 2) % NY, row % 2
    z, xhi = col // 2, col % 2

    def at_z(step):
        return (z + step + NZ) % NZ

    def at_y(step):
        return (y + step + NY) % NY

    z_up = {"row": row, "col": at_z(1) * 2 + xhi}
    z_down = {"row": row, "col": at_z(-1) * 2 + xhi}
    x_far = {"row": row, "col": z * 2 + (1 - xhi)}
    y_up = {"row": xlo * 8 + at_y(1) * 2 + core, "col": col}
    y_down = {"row": xlo * 8 + at_y(-1) * 2 + core, "col": col}
    x_near = {"row": (1 - xlo) * 8 + y * 2 + core, "col": col}
    sibling = {"row": xlo * 8 + y * 2 + (1 - core), "col": col}
    strip_up = {"row": (row + 1) % 16, "col": col}
    strip_down = {"row": (row + 15) % 16, "col": col}

    def col_peer(step):
        return {"row": row, "col": (col + step) % 16}

    counts = {"recv": 0, "send": 0}

    def take(kind):
        counts[kind] += 1
        return counts[kind] - 1

    sends = []

    def group(whole):
        sends.append((take("send"), whole))
        return sends[-1][0]

    def send(src, dst, where, sem=None, recv=None):
        if sem is None:
            sem = group(src)
        copy = pltpu.make_async_remote_copy(
            src_ref=src, dst_ref=dst, send_sem=send_sem.at[sem],
            recv_sem=recv_sem.at[take("recv") if recv is None else recv],
            device_id=where, device_id_type=MESH,
        )
        copy.start()
        return copy

    def blocks15():
        return group(xg.at[0:15])

    barrier = pltpu.get_barrier_semaphore()
    peers = [strip_up, strip_down, y_up, y_down, x_near, x_far, z_up, z_down]
    for peer in peers:
        pl.semaphore_signal(barrier, inc=1, device_id=peer, device_id_type=MESH)
    zero_edge = jnp.zeros((2, 10, LEFT, CB), F32)
    pad[:, :, 0:LEFT] = zero_edge
    pad[:, :, LEFT + 64 : 2 * LEFT + 64] = zero_edge
    pad[:, 3:7, LEFT : LEFT + 64] = images[...].astype(F32)
    for q in range(4):
        part = slice(q * 128, (q + 1) * 128)
        gg[col, part] = (cot[part].astype(F32) * lscale[...]).astype(BF16)
    wi[core, y, xlo] = w_in[...]
    wo[core, y, xlo] = w_out[...]
    pl.semaphore_wait(barrier, len(peers))

    def ring_gather(buf, half, count, sem):
        def block(zi, lo=0, n=count):
            return buf.at[zi * 2 + half, pl.ds(lo, n)]

        up = send(block(z), block(z), z_up, sem)
        down = send(block(z), block(z), z_down, sem)
        yield
        for k in (1, 2, 3):
            if k < 3:
                up.wait_recv()
                up = send(block(at_z(-k)), block(at_z(-k)), z_up, sem)
                down.wait_recv()
                down = send(block(at_z(k)), block(at_z(k)), z_down, sem)
            else:
                h = count // 2
                up.wait_recv()
                up = send(block(at_z(-3), 0, h), block(at_z(-3), 0, h), z_up, sem)
                down.wait_recv()
                down = send(block(at_z(3), h, h), block(at_z(3), h, h), z_down, sem)
            yield
        up.wait_recv()
        down.wait_recv()
        yield

    def gather_col(buf):
        sem = blocks15()
        far = []

        def rows(zi, half, first, count):
            return buf.at[zi * 2 + half, pl.ds(first, count)]

        def own():
            ring = ring_gather(buf, xhi, PIX, sem)
            near = send(rows(z, xhi, 0, n0), rows(z, xhi, 0, n0), x_far, sem)
            next(ring)
            far.append(send(rows(z, xhi, n0, n1), rows(z, xhi, n0, n1), x_far, sem))
            yield near
            for k in (1, 2, 3, 4):
                next(ring)
                for step in (-k, k) if k < 4 else (4,):
                    part = rows(at_z(step), xhi, n0, n1)
                    far.append(send(part, part, x_far, sem))
                yield

        def other(near):
            near.wait_recv()
            ring = ring_gather(buf, 1 - xhi, n0, sem)
            for k in range(5):
                next(ring)
                yield

        def rest(count):
            for copy in far[:count]:
                copy.wait_recv()
            del far[:count]

        first = own()
        second = other(next(first))
        return first, second, rest

    def gather_stats(slots):
        near = send(slots.at[0, 0], slots.at[0, 1], x_far)
        yield
        near.wait_recv()
        up = send(slots.at[0], slots.at[NZ - 1], z_up)
        down = send(slots.at[0], slots.at[1], z_down)
        yield
        for k in (1, 2, 3):
            up.wait_recv()
            up = send(slots.at[NZ - k], slots.at[NZ - k - 1], z_up)
            down.wait_recv()
            if k < 3:
                down = send(slots.at[k], slots.at[k + 1], z_down)
            yield
        up.wait_recv()
        yield

    def gather_row(buf, own):
        def block(k, yi, xi, lo=0, n=CB):
            return buf.at[k, yi, xi, pl.ds(lo, n)]
        waits = []
        sem = blocks15()

        def share(yi, xi):
            waits.append(send(block(core, yi, xi), block(core, yi, xi), sibling, sem))

        near = send(own, block(core, y, xlo), x_near, sem)
        up, down = {}, {}
        up[0] = send(own, block(core, y, xlo), y_up, sem)
        down[0] = send(own, block(core, y, xlo), y_down, sem)
        waits.append(send(own, block(core, y, xlo), sibling, sem))
        yield
        near.wait_recv()
        other = 1 - xlo
        up[1] = send(block(core, y, other), block(core, y, other), y_up, sem)
        down[1] = send(block(core, y, other), block(core, y, other), y_down, sem)
        share(y, other)
        yield
        h = CB // 2
        for i, xi in enumerate((xlo, other)):
            up[i].wait_recv()
            down[i].wait_recv()
            low, high = block(core, at_y(-1), xi, 0, h), block(core, at_y(1), xi, h, h)
            up[i] = send(low, low, y_up, sem)
            down[i] = send(high, high, y_down, sem)
            share(at_y(-1), xi)
            share(at_y(1), xi)
            yield
        for i, xi in enumerate((xlo, other)):
            up[i].wait_recv()
            down[i].wait_recv()
            share(at_y(2), xi)
        yield
        for copy in waits:
            copy.wait_recv()
        yield

    def add_into(dst, src):
        dst[...] = (dst[...].astype(F32) + src[...].astype(F32)).astype(BF16)

    def ring_scatter(buf, half, count, rm, rp, ready, sem):
        h = count // 2

        def block(zi, lo=0, n=count):
            return buf.at[zi * 2 + half, pl.ds(lo, n)]

        ready(4)
        down = send(block(at_z(-4), 0, h), rm.at[0, pl.ds(0, h)], z_down, sem)
        up = send(block(at_z(4), h, h), rp.at[0, pl.ds(0, h)], z_up, sem)
        yield
        for k in (2, 3, 4):
            dist = 5 - k
            ready(-dist)
            ready(dist)
            down.wait_recv()
            if k == 2:
                add_into(block(at_z(-dist), 0, h), rm.at[0, pl.ds(0, h)])
            else:
                add_into(block(at_z(-dist)), rm.at[k - 2])
            down = send(block(at_z(-dist)), rm.at[k - 1], z_down, sem)
            up.wait_recv()
            if k == 2:
                add_into(block(at_z(dist), h, h), rp.at[0, pl.ds(0, h)])
            else:
                add_into(block(at_z(dist)), rp.at[k - 2])
            up = send(block(at_z(dist)), rp.at[k - 1], z_up, sem)
            yield
        ready(0)
        down.wait_recv()
        up.wait_recv()
        yield

    def scatter_col(buf, rm, rp, rmo, rpo, rx, xs_, xr, total):
        sem = blocks15()
        far = {}

        def offer(step):
            zi = at_z(step)
            far[step % NZ] = send(
                buf.at[zi * 2 + 1 - xhi, pl.ds(n0, n1)], rx.at[zi], x_far, sem
            )

        def ready(step):
            zi = at_z(step)
            far[step % NZ].wait_recv()
            add_into(buf.at[zi * 2 + xhi, pl.ds(n0, n1)], rx.at[zi])

        last = []

        def other():
            half = 1 - xhi
            ring = ring_scatter(buf, half, n0, rmo, rpo, lambda step: None, sem)
            for k in range(4):
                next(ring)
                yield
            next(ring)
            xs_[...] = (
                buf[z * 2 + half, 0:n0].astype(F32) + rmo[3].astype(F32) + rpo[3].astype(F32)
            ).astype(BF16)
            last.append(send(xs_, xr, x_far, sem))
            yield

        def own():
            ring = ring_scatter(buf, xhi, PIX, rm, rp, ready, sem)
            for k in range(5):
                next(ring)
                yield
            last[0].wait_recv()
            both = buf[z * 2 + xhi].astype(F32) + rm[3].astype(F32) + rp[3].astype(F32)
            total[0:n0] = both[0:n0] + xr[...].astype(F32)
            total[n0:PIX] = both[n0:PIX]
            yield

        return offer, other(), own()

    def scatter_row(buf, rc, rm, rp, rx, xs_slot, out):
        h = CB // 2
        shared = {}
        sem = blocks15()
        for step in (2, -1, 1, 0):
            shared[step] = send(buf.at[1 - core, at_y(step)], rc.at[at_y(step)], sibling, sem)
        yield
        shared[2].wait_recv()
        add_into(buf.at[core, at_y(2)], rc.at[at_y(2)])
        down = send(
            buf.at[core, at_y(-2), :, pl.ds(0, h)], rm.at[0, :, pl.ds(0, h)], y_down, sem
        )
        up = send(buf.at[core, at_y(2), :, pl.ds(h, h)], rp.at[0, :, pl.ds(0, h)], y_up, sem)
        for step in (-1, 1, 0):
            shared[step].wait_recv()
            add_into(buf.at[core, at_y(step)], rc.at[at_y(step)])
        yield
        down.wait_recv()
        add_into(buf.at[core, at_y(-1), :, pl.ds(0, h)], rm.at[0, :, pl.ds(0, h)])
        down = send(buf.at[core, at_y(-1)], rm.at[1], y_down, sem)
        up.wait_recv()
        add_into(buf.at[core, at_y(1), :, pl.ds(h, h)], rp.at[0, :, pl.ds(0, h)])
        up = send(buf.at[core, at_y(1)], rp.at[1], y_up, sem)
        yield
        down.wait_recv()
        up.wait_recv()
        theirs = 1 - xlo
        xs_slot[0] = (
            buf[core, y, theirs].astype(F32)
            + rm[1, theirs].astype(F32)
            + rp[1, theirs].astype(F32)
        ).astype(BF16)
        near = send(xs_slot.at[0], rx.at[1], x_near, sem)
        yield
        near.wait_recv()
        out[...] = (
            buf[core, y, xlo].astype(F32)
            + rm[1, xlo].astype(F32)
            + rp[1, xlo].astype(F32)
            + rx[1].astype(F32)
        ).astype(BF16)
        yield

    def taps_sum(flipped, finish):
        def strip_row(bh, carry):
            image, line = bh // 4, bh % 4
            total = jnp.zeros((64, CB), F32)
            for i in range(KS):
                for j in range(KS):
                    tap = dwk[KS - 1 - i, pl.ds(KS - 1 - j, 1)] if flipped else dwk[i, pl.ds(j, 1)]
                    total = total + tap * pad[image, line + i, pl.ds(TAP0 + j, 64)]
            finish(bh, total)
            return carry

        lax.fori_loop(0, 8, strip_row, 0)

    def set_halo(low, high):
        pad[:, 0:3, LEFT : LEFT + 64] = jnp.where(row > 0, low[...].astype(F32), 0.0)
        pad[:, 7:10, LEFT : LEFT + 64] = jnp.where(row < 15, high[...].astype(F32), 0.0)

    lane = lax.broadcasted_iota(jnp.int32, (64, CB), 1)

    def put_sums(bh, first, second):
        tmp[pl.ds(pl.multiple_of(bh * 64, 64), 64)] = jnp.where(
            lane == 0, first, jnp.where(lane == 1, second, 0.0)
        )

    def packed_sums():
        parts = [jnp.transpose(tmp[q * 128 : (q + 1) * 128]) for q in range(4)]
        return jnp.concatenate([p[0:1] for p in parts] + [p[1:2] for p in parts], axis=0)

    def exchange_sums(slots):
        slots[col] = packed_sums()
        sem, recv = group(slots.at[0:15]), take("recv")
        for k in range(1, 16):
            send(slots.at[col], slots.at[col], col_peer(k), sem, recv)
        return pltpu.make_async_remote_copy(
            src_ref=slots.at[0:15], dst_ref=slots.at[0:15], send_sem=send_sem.at[sem],
            recv_sem=recv_sem.at[recv], device_id=col_peer(1), device_id_type=MESH,
        )

    def spread(line):
        return jnp.transpose(jnp.broadcast_to(line, (128, 128)))

    copies = [
        send(images.at[:, 1:4], halo_lo, strip_up),
        send(images.at[:, 0:3], halo_hi, strip_down),
    ]
    grads, grads2, grads_rest = gather_col(gg)
    streams = dict(G=grads, g=grads2)

    def run(order):
        for name in order:
            next(streams[name])

    run(PRE_ORDER)

    for copy in copies:
        copy.wait_recv()
    win = gather_row(wi, w_in)
    next(win)
    wout = gather_row(wo, w_out)
    next(wout)
    streams.update(W=win, w=wout)
    set_halo(halo_lo, halo_hi)

    def after_conv(bh, total):
        part = pl.ds(pl.multiple_of(bh * 64, 64), 64)
        conv[part] = total
        mean = jnp.sum(total, axis=1, keepdims=True) * (1.0 / CB)
        dev = total - mean
        xg[col, part] = dev.astype(BF16)
        put_sums(bh, mean, jnp.sum(dev * dev, axis=1, keepdims=True))

    taps_sum(False, after_conv)
    run(MID_ORDER)
    pix, pix2, pix_rest = gather_col(xg)
    st1[0, 0, 0:8] = packed_sums()
    st1[0, 0, 8:16] = jnp.broadcast_to(gain[...], (8, CB))
    stats = gather_stats(st1)
    next(stats)

    def pair(buf, zi):
        return jnp.concatenate([buf[zi * 2], buf[zi * 2 + 1]], axis=1)

    def panel(buf, zi):
        xi, yi = zi // NY, zi % NY
        return jnp.concatenate([buf[0, yi, xi], buf[1, yi, xi]], axis=0)

    def product(acc, buf, weight, step, first):
        zi = at_z(step)
        term = jnp.dot(pair(buf, zi), panel(weight, zi), preferred_element_type=F32)
        if first:
            acc[...] = term
        else:
            acc[...] += term

    def statistics():
        every = st1[...]
        means, devs = every[:, :, 0:4], every[:, :, 4:8]
        mean = jnp.sum(means, axis=(0, 1)) * (1.0 / 16)
        shift = means - mean[None, None]
        var = (jnp.sum(devs, axis=(0, 1)) + CB * jnp.sum(shift * shift, axis=(0, 1))) * (1.0 / C)
        inv = lax.rsqrt(var + 1e-06)
        for q in range(4):
            part = slice(q * 128, (q + 1) * 128)
            lines = [shift[o, i, q : q + 1] for o in range(NZ) for i in range(2)]
            lines += [inv[q : q + 1], mean[q : q + 1], jnp.zeros((110, 128), F32)]
            turned = jnp.transpose(jnp.concatenate(lines, axis=0))
            cols[q] = turned
            scale = jnp.broadcast_to(turned[:, 16:17], (128, CB))
            istd[part] = scale
            normed[part] = (conv[part] - turned[:, 17:18]) * scale

    def gain_product(step, first):
        mine, theirs = st1[step % NZ, 0, 8:16], st1[step % NZ, 1, 8:16]
        gains = jnp.concatenate(
            [jnp.where(xhi == 0, mine, theirs), jnp.where(xhi == 0, theirs, mine)], axis=1
        )
        high = gains.astype(BF16)
        low = (gains - high.astype(F32)).astype(BF16)
        parts = jnp.concatenate([high, low], axis=0)
        term = jnp.dot(parts, panel(wi, at_z(step)), preferred_element_type=F32)
        term = term[0:8] + term[8:16]
        if first:
            gw[...] = term
        else:
            gw[...] += term

    def normalise(step):
        for other in (0, 1):
            slot = (step % NZ, other)
            half = xhi if other == 0 else 1 - xhi
            place = slot[0] * 2 + other
            scale = st1[slot[0], other, 8:9]
            for q in range(4):
                part = slice(q * 128, (q + 1) * 128)
                dev = xg[at_z(step) * 2 + half, part].astype(F32)
                value = (dev + cols[q, :, place : place + 1]) * istd[part] * scale
                xs[at_z(step) * 2 + half, part] = value.astype(BF16)

    around = (0, 1, -1, 2, -2, 3, -3, 4)

    def grad_hidden():
        grads_rest(8)
        for step in around:
            product(gh, gg, wo, step, step == 0)

    def finish_stats():
        statistics()
        for step in around:
            gain_product(step, step == 0)

    def pre_activation(distance):
        steps = around[max(0, 2 * distance - 1) : 2 * distance + 1]
        pix_rest(len(steps))
        for step in steps:
            normalise(step)
            product(hp, xs, wi, step, step == 0)

    def run(order):
        work = {"p": grad_hidden, "q": finish_stats}
        for name in order:
            if name in "01234":
                pre_activation(int(name))
            elif name in work:
                work[name]()
            else:
                next(streams[name])

    streams.update(X=pix, x=pix2, S=stats)
    run(GATHER_ORDER)

    def activate(i, carry):
        part = pl.ds(pl.multiple_of(i * 64, 64), 64)
        v = hp[part]
        cdf = 0.5 * (1.0 + lax.erf(v * 0.7071067811865476))
        slope = cdf + v * jnp.exp(-0.5 * v * v) * 0.3989422804014327
        hid[part] = (v * cdf).astype(BF16)
        grad = (gh[part] * slope).astype(BF16)
        gpre[part] = grad
        grad = grad.astype(F32)
        put_sums(
            i,
            jnp.sum(grad * gw[0:1], axis=1, keepdims=True),
            jnp.sum(grad * v, axis=1, keepdims=True),
        )
        return carry

    lax.fori_loop(0, 8, activate, 0)

    def to_channels(dst, act, weight, step):
        zi = at_z(step)
        term = lax.dot_general(
            act[...], panel(weight, zi), CONTRACT_LAST, preferred_element_type=F32
        ).astype(BF16)
        dst[zi * 2] = term[:, 0:CB]
        dst[zi * 2 + 1] = term[:, CB : 2 * CB]

    def weight_grad(dst, buf, act):
        def one(zi, carry):
            xi, yi = zi // NY, zi % NY
            term = lax.dot_general(
                pair(buf, zi), act[...], CONTRACT_FIRST, preferred_element_type=F32
            ).astype(BF16)
            dst[0, yi, xi] = term[0:CB]
            dst[1, yi, xi] = term[CB : 2 * CB]
            return carry

        lax.fori_loop(0, NZ, one, 0)

    steps = (4, -3, 3, -2, 2, -1, 1, 0)
    offer_b, back2, back = scatter_col(bk, bk_m, bk_p, bk_mo, bk_po, bk_x, bk_xs, bk_xr, gs)
    offer_c, branch2, branch = scatter_col(
        cb, cb_m, cb_p, cb_mo, cb_po, cb_x, cb_xs, cb_xr, hp.at[:, 0:CB]
    )
    for step in steps:
        to_channels(bk, gpre, wi, step)
        offer_b(step)
        if step == 4:
            next(back2)
    totals = exchange_sums(st2)
    streams = dict(
        b=back2, B=back, c=branch2, C=branch,
        M=scatter_row(g2, g2_c, g2_m, g2_p, g2_r, g2_r, gp_out),
        N=scatter_row(g1, g1_c, g1_m, g1_p, g1_r, g1_r, gp_in),
    )

    def contrib():
        for step in steps:
            to_channels(cb, hid, wo, step)
            offer_c(step)
            if step == 4:
                next(branch2)

    def run(order):
        for name in order:
            if name == "k":
                contrib()
            elif name == "m":
                weight_grad(g2, gg, hid)
            elif name == "n":
                weight_grad(g1, xs, gpre)
            elif name == "s":
                norm_terms()
            else:
                next(streams[name])

    def norm_terms():
        totals.wait_recv()
        total = jnp.sum(st2[...], axis=0) * (1.0 / C)
        for q in range(4):
            part = slice(q * 128, (q + 1) * 128)
            less[part] = istd[part] * (
                spread(total[q : q + 1]) + normed[part] * spread(total[4 + q : 5 + q])
            )

    run(BACK_ORDER)

    for q in range(4):
        part = slice(q * 128, (q + 1) * 128)
        value = istd[part] * (gs[part] * gain[...]) - less[part]
        image, line = q // 2, 2 * (q % 2)
        value = value.reshape(2, 64, CB)
        pad[image, 3 + line : 5 + line, LEFT : LEFT + 64] = value
        value = value.astype(BF16)
        if line == 0:
            edge_hi[image, 0:2] = value
            edge_lo[image, 0:1] = value[1:2]
        else:
            edge_hi[image, 2:3] = value[0:1]
            edge_lo[image, 1:3] = value
    copies = [send(edge_lo, ghalo_lo, strip_up), send(edge_hi, ghalo_hi, strip_down)]
    run(HALO_ORDER)
    for copy in copies:
        copy.wait_recv()
    set_halo(ghalo_lo, ghalo_hi)

    def after_transposed(bh, total):
        part = pl.ds(pl.multiple_of(bh * 64, 64), 64)
        grad_images[bh // 4, bh % 4] = (cot[part].astype(F32) + total).astype(BF16)

    taps_sum(True, after_transposed)

    run(LAST_ORDER)
    branch_sum = hp.at[:, 0:CB]
    for q in range(8):
        part = slice(q * 64, (q + 1) * 64)
        image, line = q // 4, q % 4
        block_out[image, line] = (
            images[image, line].astype(F32) + lscale[...] * branch_sum[part]
        ).astype(BF16)
    for sem, whole in sends:
        pltpu.make_async_remote_copy(
            src_ref=whole, dst_ref=whole, send_sem=send_sem.at[sem], recv_sem=recv_sem.at[0],
            device_id=z_up, device_id_type=MESH,
        ).wait_send()
    assert counts["recv"] <= N_RECV and counts["send"] <= N_SEND, counts
    for name, stream in streams.items():
        assert next(stream, None) is None, name


def hand_out(*refs):
    for i in range(4):
        refs[4 + i][...] = refs[i][...]


def on_device(images, dw_kernel, norm_gain, proj_in, proj_out, layer_scale, cotangent):
    n0 = 224
    n1 = PIX - n0
    strip = images.shape
    vmem = pltpu.VMEM
    col_blocks = vmem((2 * NZ, PIX, CB), BF16)
    row_blocks = vmem((2, NY, 2, CB, HB), BF16)
    scratch = (
        [vmem((2, 10, 64 + 2 * LEFT, CB), F32)]
        + [vmem((2, 3, 64, CB), BF16)] * 6
        + [vmem((PIX, CB), F32)] * 4
        + [vmem((NZ, 2, 16, CB), F32), vmem((16, 8, CB), F32), vmem((4, 128, 128), F32)]
        + [col_blocks] * 3
        + [row_blocks] * 2
        + [vmem((PIX, HB), F32)] * 2
        + [vmem((PIX, HB), BF16)] * 2
        + [vmem((PIX, CB), F32), vmem((8, HB), F32)]
        + [col_blocks] * 2
        + [vmem((4, PIX, CB), BF16)] * 4
        + [vmem((4, n0, CB), BF16)] * 4
        + [vmem((NZ, n1, CB), BF16)] * 2
        + [vmem((n0, CB), BF16)] * 4
        + [vmem((PIX, CB), F32)]
        + [row_blocks] * 2
        + [vmem((NY, 2, CB, HB), BF16)] * 2
        + [vmem((2, 2, CB, HB), BF16)] * 4
        + [vmem((2, CB, HB), BF16)] * 2
        + [pltpu.SemaphoreType.DMA((N_SEND,)), pltpu.SemaphoreType.DMA((N_RECV,))]
    )
    block = pl.BlockSpec(memory_space=pltpu.VMEM)
    outs = pl.pallas_call(
        functools.partial(kernel, n0),
        out_shape=(
            jax.ShapeDtypeStruct(strip, BF16),
            jax.ShapeDtypeStruct(strip, BF16),
            jax.ShapeDtypeStruct(proj_in.shape, BF16),
            jax.ShapeDtypeStruct(proj_out.shape, BF16),
        ),
        in_specs=[block] * 7,
        out_specs=(block,) * 4,
        scratch_shapes=scratch,
        compiler_params=pltpu.CompilerParams(
            collective_id=0, has_side_effects=True, vmem_limit_bytes=56 << 20
        ),
    )(
        images,
        dw_kernel,
        norm_gain.reshape(1, CB),
        proj_in,
        proj_out,
        layer_scale.reshape(1, CB),
        cotangent.reshape(PIX, CB),
    )
    return pl.pallas_call(
        hand_out,
        out_shape=tuple(jax.ShapeDtypeStruct(out.shape, out.dtype) for out in outs),
        in_specs=[block] * 4,
        out_specs=(block,) * 4,
    )(*outs)


def solution(mesh):
    placed = (
        P(None, "row", None, "col"),
        P(None, None, "col"),
        P("col"),
        P("row", "col"),
        P("row", "col"),
        P("col"),
        P(None, "row", None, "col"),
    )
    return jax.shard_map(
        on_device,
        mesh=mesh,
        in_specs=placed,
        out_specs=(
            P(None, "row", None, "col"),
            P(None, "row", None, "col"),
            P("row", "col"),
            P("row", "col"),
        ),
        check_vma=False,
    )
```

```python
import functools

import jax
import jax.numpy as jnp
from jax import lax
from jax.experimental import pallas as pl
from jax.experimental.pallas import tpu as pltpu
from jax.sharding import PartitionSpec as P

MESH = pl.DeviceIdType.MESH
F32, BF16 = jnp.float32, jnp.bfloat16
C = 2048
KS = 7
NZ, NY = 8, 4
CB = 128
HB = 512
PIX = 512
LEFT = 8
TAP0 = LEFT - KS // 2
N_SEND, N_RECV = 21, 165
PRE_ORDER = ""
MID_ORDER = ""
GATHER_ORDER = "gGxXSgGSxXWwgGWwSxXWwgGWwSxXgWwpSq012x34"
BACK_ORDER = "mMBnNbBkMbBcCNbBcCMsbBNB"
HALO_ORDER = "cCMN"
MIDDLE_ORDER = "cC"
LAST_ORDER = "MNCC"
CONTRACT_LAST = (((1,), (1,)), ((), ()))
CONTRACT_FIRST = (((0,), (0,)), ((), ()))


def kernel(
    n0,
    images, dwk, gain, w_in, w_out, lscale, cot,
    block_out, grad_images, gp_in, gp_out,
    pad, halo_lo, halo_hi, ghalo_lo, ghalo_hi, edge_lo, edge_hi,
    conv, normed, istd, tmp, st1, st2,
    cols, xg, xs, gg, wi, wo, hp, gh, hid, gpre,
    less, gw, cb, bk, cb_m, cb_p, bk_m, bk_p, cb_mo, cb_po, bk_mo, bk_po,
    cb_x, bk_x, cb_xs, bk_xs, cb_xr, bk_xr, gs,
    g1, g2, g1_c, g2_c, g1_m, g1_p, g2_m, g2_p, g1_r, g2_r,
    send_sem, recv_sem,
):
    n1 = PIX - n0
    row, col = lax.axis_index("row"), lax.axis_index("col")
    xlo, y, core = row // 8, (row // 2) % NY, row % 2
    z, xhi = col // 2, col % 2

    def at_z(step):
        return (z + step + NZ) % NZ

    def at_y(step):
        return (y + step + NY) % NY

    z_up = {"row": row, "col": at_z(1) * 2 + xhi}
    z_down = {"row": row, "col": at_z(-1) * 2 + xhi}
    x_far = {"row": row, "col": z * 2 + (1 - xhi)}
    y_up = {"row": xlo * 8 + at_y(1) * 2 + core, "col": col}
    y_down = {"row": xlo * 8 + at_y(-1) * 2 + core, "col": col}
    x_near = {"row": (1 - xlo) * 8 + y * 2 + core, "col": col}
    sibling = {"row": xlo * 8 + y * 2 + (1 - core), "col": col}
    strip_up = {"row": (row + 1) % 16, "col": col}
    strip_down = {"row": (row + 15) % 16, "col": col}

    def col_peer(step):
        return {"row": row, "col": (col + step) % 16}

    counts = {"recv": 0, "send": 0}

    def take(kind):
        counts[kind] += 1
        return counts[kind] - 1

    sends = []

    def group(whole):
        sends.append((take("send"), whole))
        return sends[-1][0]

    def send(src, dst, where, sem=None, recv=None):
        if sem is None:
            sem = group(src)
        copy = pltpu.make_async_remote_copy(
            src_ref=src, dst_ref=dst, send_sem=send_sem.at[sem],
            recv_sem=recv_sem.at[take("recv") if recv is None else recv],
            device_id=where, device_id_type=MESH,
        )
        copy.start()
        return copy

    def blocks15():
        return group(xg.at[0:15])

    barrier = pltpu.get_barrier_semaphore()
    peers = [strip_up, strip_down, y_up, y_down, x_near, x_far, z_up, z_down]
    for peer in peers:
        pl.semaphore_signal(barrier, inc=1, device_id=peer, device_id_type=MESH)
    zero_edge = jnp.zeros((2, 10, LEFT, CB), F32)
    pad[:, :, 0:LEFT] = zero_edge
    pad[:, :, LEFT + 64 : 2 * LEFT + 64] = zero_edge
    pad[:, 3:7, LEFT : LEFT + 64] = images[...].astype(F32)
    for q in range(4):
        part = slice(q * 128, (q + 1) * 128)
        gg[col, part] = (cot[part].astype(F32) * lscale[...]).astype(BF16)
    wi[core, y, xlo] = w_in[...]
    wo[core, y, xlo] = w_out[...]
    pl.semaphore_wait(barrier, len(peers))

    def ring_gather(buf, half, count, sem):
        def block(zi, lo=0, n=count):
            return buf.at[zi * 2 + half, pl.ds(lo, n)]

        up = send(block(z), block(z), z_up, sem)
        down = send(block(z), block(z), z_down, sem)
        yield
        for k in (1, 2, 3):
            if k < 3:
                up.wait_recv()
                up = send(block(at_z(-k)), block(at_z(-k)), z_up, sem)
                down.wait_recv()
                down = send(block(at_z(k)), block(at_z(k)), z_down, sem)
            else:
                h = count // 2
                up.wait_recv()
                up = send(block(at_z(-3), 0, h), block(at_z(-3), 0, h), z_up, sem)
                down.wait_recv()
                down = send(block(at_z(3), h, h), block(at_z(3), h, h), z_down, sem)
            yield
        up.wait_recv()
        down.wait_recv()
        yield

    def gather_col(buf):
        sem = blocks15()
        far = []

        def rows(zi, half, first, count):
            return buf.at[zi * 2 + half, pl.ds(first, count)]

        def own():
            ring = ring_gather(buf, xhi, PIX, sem)
            near = send(rows(z, xhi, 0, n0), rows(z, xhi, 0, n0), x_far, sem)
            next(ring)
            far.append(send(rows(z, xhi, n0, n1), rows(z, xhi, n0, n1), x_far, sem))
            yield near
            for k in (1, 2, 3, 4):
                next(ring)
                for step in (-k, k) if k < 4 else (4,):
                    part = rows(at_z(step), xhi, n0, n1)
                    far.append(send(part, part, x_far, sem))
                yield

        def other(near):
            near.wait_recv()
            ring = ring_gather(buf, 1 - xhi, n0, sem)
            for k in range(5):
                next(ring)
                yield

        def rest(count):
            for copy in far[:count]:
                copy.wait_recv()
            del far[:count]

        first = own()
        second = other(next(first))
        return first, second, rest

    def gather_stats(slots):
        near = send(slots.at[0, 0], slots.at[0, 1], x_far)
        yield
        near.wait_recv()
        up = send(slots.at[0], slots.at[NZ - 1], z_up)
        down = send(slots.at[0], slots.at[1], z_down)
        yield
        for k in (1, 2, 3):
            up.wait_recv()
            up = send(slots.at[NZ - k], slots.at[NZ - k - 1], z_up)
            down.wait_recv()
            if k < 3:
                down = send(slots.at[k], slots.at[k + 1], z_down)
            yield
        up.wait_recv()
        yield

    def gather_row(buf, own):
        def block(k, yi, xi, lo=0, n=CB):
            return buf.at[k, yi, xi, pl.ds(lo, n)]
        waits = []
        sem = blocks15()

        def share(yi, xi):
            waits.append(send(block(core, yi, xi), block(core, yi, xi), sibling, sem))

        near = send(own, block(core, y, xlo), x_near, sem)
        up, down = {}, {}
        up[0] = send(own, block(core, y, xlo), y_up, sem)
        down[0] = send(own, block(core, y, xlo), y_down, sem)
        waits.append(send(own, block(core, y, xlo), sibling, sem))
        yield
        near.wait_recv()
        other = 1 - xlo
        up[1] = send(block(core, y, other), block(core, y, other), y_up, sem)
        down[1] = send(block(core, y, other), block(core, y, other), y_down, sem)
        share(y, other)
        yield
        h = CB // 2
        for i, xi in enumerate((xlo, other)):
            up[i].wait_recv()
            down[i].wait_recv()
            low, high = block(core, at_y(-1), xi, 0, h), block(core, at_y(1), xi, h, h)
            up[i] = send(low, low, y_up, sem)
            down[i] = send(high, high, y_down, sem)
            share(at_y(-1), xi)
            share(at_y(1), xi)
            yield
        for i, xi in enumerate((xlo, other)):
            up[i].wait_recv()
            down[i].wait_recv()
            share(at_y(2), xi)
        yield
        for copy in waits:
            copy.wait_recv()
        yield

    def add_into(dst, src):
        dst[...] = (dst[...].astype(F32) + src[...].astype(F32)).astype(BF16)

    def ring_scatter(buf, half, count, rm, rp, ready, sem):
        h = count // 2

        def block(zi, lo=0, n=count):
            return buf.at[zi * 2 + half, pl.ds(lo, n)]

        ready(4)
        down = send(block(at_z(-4), 0, h), rm.at[0, pl.ds(0, h)], z_down, sem)
        up = send(block(at_z(4), h, h), rp.at[0, pl.ds(0, h)], z_up, sem)
        yield
        for k in (2, 3, 4):
            dist = 5 - k
            ready(-dist)
            ready(dist)
            down.wait_recv()
            if k == 2:
                add_into(block(at_z(-dist), 0, h), rm.at[0, pl.ds(0, h)])
            else:
                add_into(block(at_z(-dist)), rm.at[k - 2])
            down = send(block(at_z(-dist)), rm.at[k - 1], z_down, sem)
            up.wait_recv()
            if k == 2:
                add_into(block(at_z(dist), h, h), rp.at[0, pl.ds(0, h)])
            else:
                add_into(block(at_z(dist)), rp.at[k - 2])
            up = send(block(at_z(dist)), rp.at[k - 1], z_up, sem)
            yield
        ready(0)
        down.wait_recv()
        up.wait_recv()
        yield

    def scatter_col(buf, rm, rp, rmo, rpo, rx, xs_, xr, total):
        sem = blocks15()
        far = {}

        def offer(step):
            zi = at_z(step)
            far[step % NZ] = send(
                buf.at[zi * 2 + 1 - xhi, pl.ds(n0, n1)], rx.at[zi], x_far, sem
            )

        def ready(step):
            zi = at_z(step)
            far[step % NZ].wait_recv()
            add_into(buf.at[zi * 2 + xhi, pl.ds(n0, n1)], rx.at[zi])

        last = []

        def other():
            half = 1 - xhi
            ring = ring_scatter(buf, half, n0, rmo, rpo, lambda step: None, sem)
            for k in range(4):
                next(ring)
                yield
            next(ring)
            xs_[...] = (
                buf[z * 2 + half, 0:n0].astype(F32) + rmo[3].astype(F32) + rpo[3].astype(F32)
            ).astype(BF16)
            last.append(send(xs_, xr, x_far, sem))
            yield

        def own():
            ring = ring_scatter(buf, xhi, PIX, rm, rp, ready, sem)
            for k in range(5):
                next(ring)
                yield
            last[0].wait_recv()
            both = buf[z * 2 + xhi].astype(F32) + rm[3].astype(F32) + rp[3].astype(F32)
            total[0:n0] = both[0:n0] + xr[...].astype(F32)
            total[n0:PIX] = both[n0:PIX]
            yield

        return offer, other(), own()

    def scatter_row(buf, rc, rm, rp, rx, xs_slot, out):
        h = CB // 2
        shared = {}
        sem = blocks15()
        for step in (2, -1, 1, 0):
            shared[step] = send(buf.at[1 - core, at_y(step)], rc.at[at_y(step)], sibling, sem)
        yield
        shared[2].wait_recv()
        add_into(buf.at[core, at_y(2)], rc.at[at_y(2)])
        down = send(
            buf.at[core, at_y(-2), :, pl.ds(0, h)], rm.at[0, :, pl.ds(0, h)], y_down, sem
        )
        up = send(buf.at[core, at_y(2), :, pl.ds(h, h)], rp.at[0, :, pl.ds(0, h)], y_up, sem)
        for step in (-1, 1, 0):
            shared[step].wait_recv()
            add_into(buf.at[core, at_y(step)], rc.at[at_y(step)])
        yield
        down.wait_recv()
        add_into(buf.at[core, at_y(-1), :, pl.ds(0, h)], rm.at[0, :, pl.ds(0, h)])
        down = send(buf.at[core, at_y(-1)], rm.at[1], y_down, sem)
        up.wait_recv()
        add_into(buf.at[core, at_y(1), :, pl.ds(h, h)], rp.at[0, :, pl.ds(0, h)])
        up = send(buf.at[core, at_y(1)], rp.at[1], y_up, sem)
        yield
        down.wait_recv()
        up.wait_recv()
        theirs = 1 - xlo
        xs_slot[0] = (
            buf[core, y, theirs].astype(F32)
            + rm[1, theirs].astype(F32)
            + rp[1, theirs].astype(F32)
        ).astype(BF16)
        near = send(xs_slot.at[0], rx.at[1], x_near, sem)
        yield
        near.wait_recv()
        out[...] = (
            buf[core, y, xlo].astype(F32)
            + rm[1, xlo].astype(F32)
            + rp[1, xlo].astype(F32)
            + rx[1].astype(F32)
        ).astype(BF16)
        yield

    def taps_sum(flipped, finish):
        def strip_row(bh, carry):
            image, line = bh // 4, bh % 4
            total = jnp.zeros((64, CB), F32)
            for i in range(KS):
                for j in range(KS):
                    tap = dwk[KS - 1 - i, pl.ds(KS - 1 - j, 1)] if flipped else dwk[i, pl.ds(j, 1)]
                    total = total + tap * pad[image, line + i, pl.ds(TAP0 + j, 64)]
            finish(bh, total)
            return carry

        lax.fori_loop(0, 8, strip_row, 0)

    def set_halo(low, high):
        pad[:, 0:3, LEFT : LEFT + 64] = jnp.where(row > 0, low[...].astype(F32), 0.0)
        pad[:, 7:10, LEFT : LEFT + 64] = jnp.where(row < 15, high[...].astype(F32), 0.0)

    lane = lax.broadcasted_iota(jnp.int32, (64, CB), 1)

    def put_sums(bh, first, second):
        tmp[pl.ds(pl.multiple_of(bh * 64, 64), 64)] = jnp.where(
            lane == 0, first, jnp.where(lane == 1, second, 0.0)
        )

    def packed_sums():
        parts = [jnp.transpose(tmp[q * 128 : (q + 1) * 128]) for q in range(4)]
        return jnp.concatenate([p[0:1] for p in parts] + [p[1:2] for p in parts], axis=0)

    def exchange_sums(slots):
        slots[col] = packed_sums()
        sem, recv = group(slots.at[0:15]), take("recv")
        for k in range(1, 16):
            send(slots.at[col], slots.at[col], col_peer(k), sem, recv)
        return pltpu.make_async_remote_copy(
            src_ref=slots.at[0:15], dst_ref=slots.at[0:15], send_sem=send_sem.at[sem],
            recv_sem=recv_sem.at[recv], device_id=col_peer(1), device_id_type=MESH,
        )

    def spread(line):
        return jnp.transpose(jnp.broadcast_to(line, (128, 128)))

    copies = [
        send(images.at[:, 1:4], halo_lo, strip_up),
        send(images.at[:, 0:3], halo_hi, strip_down),
    ]
    grads, grads2, grads_rest = gather_col(gg)
    streams = dict(G=grads, g=grads2)

    def run(order):
        for name in order:
            next(streams[name])

    run(PRE_ORDER)

    for copy in copies:
        copy.wait_recv()
    win = gather_row(wi, w_in)
    next(win)
    wout = gather_row(wo, w_out)
    next(wout)
    streams.update(W=win, w=wout)
    set_halo(halo_lo, halo_hi)

    def after_conv(bh, total):
        part = pl.ds(pl.multiple_of(bh * 64, 64), 64)
        conv[part] = total
        mean = jnp.sum(total, axis=1, keepdims=True) * (1.0 / CB)
        dev = total - mean
        xg[col, part] = dev.astype(BF16)
        put_sums(bh, mean, jnp.sum(dev * dev, axis=1, keepdims=True))

    taps_sum(False, after_conv)
    run(MID_ORDER)
    pix, pix2, pix_rest = gather_col(xg)
    st1[0, 0, 0:8] = packed_sums()
    st1[0, 0, 8:16] = jnp.broadcast_to(gain[...], (8, CB))
    stats = gather_stats(st1)
    next(stats)

    def pair(buf, zi):
        return jnp.concatenate([buf[zi * 2], buf[zi * 2 + 1]], axis=1)

    def panel(buf, zi):
        xi, yi = zi // NY, zi % NY
        return jnp.concatenate([buf[0, yi, xi], buf[1, yi, xi]], axis=0)

    def product(acc, buf, weight, step, first):
        zi = at_z(step)
        term = jnp.dot(pair(buf, zi), panel(weight, zi), preferred_element_type=F32)
        if first:
            acc[...] = term
        else:
            acc[...] += term

    def statistics():
        every = st1[...]
        means, devs = every[:, :, 0:4], every[:, :, 4:8]
        mean = jnp.sum(means, axis=(0, 1)) * (1.0 / 16)
        shift = means - mean[None, None]
        var = (jnp.sum(devs, axis=(0, 1)) + CB * jnp.sum(shift * shift, axis=(0, 1))) * (1.0 / C)
        inv = lax.rsqrt(var + 1e-06)
        for q in range(4):
            part = slice(q * 128, (q + 1) * 128)
            lines = [shift[o, i, q : q + 1] for o in range(NZ) for i in range(2)]
            lines += [inv[q : q + 1], mean[q : q + 1], jnp.zeros((110, 128), F32)]
            turned = jnp.transpose(jnp.concatenate(lines, axis=0))
            cols[q] = turned
            scale = jnp.broadcast_to(turned[:, 16:17], (128, CB))
            istd[part] = scale
            normed[part] = (conv[part] - turned[:, 17:18]) * scale

    def gain_product(step, first):
        mine, theirs = st1[step % NZ, 0, 8:16], st1[step % NZ, 1, 8:16]
        gains = jnp.concatenate(
            [jnp.where(xhi == 0, mine, theirs), jnp.where(xhi == 0, theirs, mine)], axis=1
        )
        high = gains.astype(BF16)
        low = (gains - high.astype(F32)).astype(BF16)
        parts = jnp.concatenate([high, low], axis=0)
        term = jnp.dot(parts, panel(wi, at_z(step)), preferred_element_type=F32)
        term = term[0:8] + term[8:16]
        if first:
            gw[...] = term
        else:
            gw[...] += term

    def normalise(step):
        for other in (0, 1):
            slot = (step % NZ, other)
            half = xhi if other == 0 else 1 - xhi
            place = slot[0] * 2 + other
            scale = st1[slot[0], other, 8:9]
            for q in range(4):
                part = slice(q * 128, (q + 1) * 128)
                dev = xg[at_z(step) * 2 + half, part].astype(F32)
                value = (dev + cols[q, :, place : place + 1]) * istd[part] * scale
                xs[at_z(step) * 2 + half, part] = value.astype(BF16)

    around = (0, 1, -1, 2, -2, 3, -3, 4)

    def grad_hidden():
        grads_rest(8)
        for step in around:
            product(gh, gg, wo, step, step == 0)

    def finish_stats():
        statistics()
        for step in around:
            gain_product(step, step == 0)

    def pre_activation(distance):
        steps = around[max(0, 2 * distance - 1) : 2 * distance + 1]
        pix_rest(len(steps))
        for step in steps:
            normalise(step)
            product(hp, xs, wi, step, step == 0)

    def run(order):
        work = {"p": grad_hidden, "q": finish_stats}
        for name in order:
            if name in "01234":
                pre_activation(int(name))
            elif name in work:
                work[name]()
            else:
                next(streams[name])

    streams.update(X=pix, x=pix2, S=stats)
    run(GATHER_ORDER)

    def activate(i, carry):
        part = pl.ds(pl.multiple_of(i * 64, 64), 64)
        v = hp[part]
        cdf = 0.5 * (1.0 + lax.erf(v * 0.7071067811865476))
        slope = cdf + v * jnp.exp(-0.5 * v * v) * 0.3989422804014327
        hid[part] = (v * cdf).astype(BF16)
        grad = (gh[part] * slope).astype(BF16)
        gpre[part] = grad
        grad = grad.astype(F32)
        put_sums(
            i,
            jnp.sum(grad * gw[0:1], axis=1, keepdims=True),
            jnp.sum(grad * v, axis=1, keepdims=True),
        )
        return carry

    lax.fori_loop(0, 8, activate, 0)

    def to_channels(dst, act, weight, step):
        zi = at_z(step)
        term = lax.dot_general(
            act[...], panel(weight, zi), CONTRACT_LAST, preferred_element_type=F32
        ).astype(BF16)
        dst[zi * 2] = term[:, 0:CB]
        dst[zi * 2 + 1] = term[:, CB : 2 * CB]

    def weight_grad(dst, buf, act):
        def one(zi, carry):
            xi, yi = zi // NY, zi % NY
            term = lax.dot_general(
                pair(buf, zi), act[...], CONTRACT_FIRST, preferred_element_type=F32
            ).astype(BF16)
            dst[0, yi, xi] = term[0:CB]
            dst[1, yi, xi] = term[CB : 2 * CB]
            return carry

        lax.fori_loop(0, NZ, one, 0)

    steps = (4, -3, 3, -2, 2, -1, 1, 0)
    offer_b, back2, back = scatter_col(bk, bk_m, bk_p, bk_mo, bk_po, bk_x, bk_xs, bk_xr, gs)
    offer_c, branch2, branch = scatter_col(
        cb, cb_m, cb_p, cb_mo, cb_po, cb_x, cb_xs, cb_xr, hp.at[:, 0:CB]
    )
    for step in steps:
        to_channels(bk, gpre, wi, step)
        offer_b(step)
        if step == 4:
            next(back2)
    totals = exchange_sums(st2)
    streams = dict(
        b=back2, B=back, c=branch2, C=branch,
        M=scatter_row(g2, g2_c, g2_m, g2_p, g2_r, g2_r, gp_out),
        N=scatter_row(g1, g1_c, g1_m, g1_p, g1_r, g1_r, gp_in),
    )

    def contrib():
        for step in steps:
            to_channels(cb, hid, wo, step)
            offer_c(step)
            if step == 4:
                next(branch2)

    def run(order):
        for name in order:
            if name == "k":
                contrib()
            elif name == "m":
                weight_grad(g2, gg, hid)
            elif name == "n":
                weight_grad(g1, xs, gpre)
            elif name == "s":
                norm_terms()
            else:
                next(streams[name])

    def norm_terms():
        totals.wait_recv()
        total = jnp.sum(st2[...], axis=0) * (1.0 / C)
        for q in range(4):
            part = slice(q * 128, (q + 1) * 128)
            less[part] = istd[part] * (
                spread(total[q : q + 1]) + normed[part] * spread(total[4 + q : 5 + q])
            )

    run(BACK_ORDER)

    for q in range(4):
        part = slice(q * 128, (q + 1) * 128)
        value = istd[part] * (gs[part] * gain[...]) - less[part]
        image, line = q // 2, 2 * (q % 2)
        value = value.reshape(2, 64, CB)
        pad[image, 3 + line : 5 + line, LEFT : LEFT + 64] = value
        value = value.astype(BF16)
        if line == 0:
            edge_hi[image, 0:2] = value
            edge_lo[image, 0:1] = value[1:2]
        else:
            edge_hi[image, 2:3] = value[0:1]
            edge_lo[image, 1:3] = value
    copies = [send(edge_lo, ghalo_lo, strip_up), send(edge_hi, ghalo_hi, strip_down)]
    run(HALO_ORDER)
    for copy in copies:
        copy.wait_recv()
    set_halo(ghalo_lo, ghalo_hi)
    run(MIDDLE_ORDER)

    def after_transposed(bh, total):
        part = pl.ds(pl.multiple_of(bh * 64, 64), 64)
        grad_images[bh // 4, bh % 4] = (cot[part].astype(F32) + total).astype(BF16)

    taps_sum(True, after_transposed)

    run(LAST_ORDER)
    branch_sum = hp.at[:, 0:CB]
    for q in range(8):
        part = slice(q * 64, (q + 1) * 64)
        image, line = q // 4, q % 4
        block_out[image, line] = (
            images[image, line].astype(F32) + lscale[...] * branch_sum[part]
        ).astype(BF16)
    for sem, whole in sends:
        pltpu.make_async_remote_copy(
            src_ref=whole, dst_ref=whole, send_sem=send_sem.at[sem], recv_sem=recv_sem.at[0],
            device_id=z_up, device_id_type=MESH,
        ).wait_send()
    assert counts["recv"] <= N_RECV and counts["send"] <= N_SEND, counts
    for name, stream in streams.items():
        assert next(stream, None) is None, name


def hand_out(*refs):
    for i in range(4):
        refs[4 + i][...] = refs[i][...]


def on_device(images, dw_kernel, norm_gain, proj_in, proj_out, layer_scale, cotangent):
    n0 = 224
    n1 = PIX - n0
    strip = images.shape
    vmem = pltpu.VMEM
    col_blocks = vmem((2 * NZ, PIX, CB), BF16)
    row_blocks = vmem((2, NY, 2, CB, HB), BF16)
    scratch = (
        [vmem((2, 10, 64 + 2 * LEFT, CB), F32)]
        + [vmem((2, 3, 64, CB), BF16)] * 6
        + [vmem((PIX, CB), F32)] * 4
        + [vmem((NZ, 2, 16, CB), F32), vmem((16, 8, CB), F32), vmem((4, 128, 128), F32)]
        + [col_blocks] * 3
        + [row_blocks] * 2
        + [vmem((PIX, HB), F32)] * 2
        + [vmem((PIX, HB), BF16)] * 2
        + [vmem((PIX, CB), F32), vmem((8, HB), F32)]
        + [col_blocks] * 2
        + [vmem((4, PIX, CB), BF16)] * 4
        + [vmem((4, n0, CB), BF16)] * 4
        + [vmem((NZ, n1, CB), BF16)] * 2
        + [vmem((n0, CB), BF16)] * 4
        + [vmem((PIX, CB), F32)]
        + [row_blocks] * 2
        + [vmem((NY, 2, CB, HB), BF16)] * 2
        + [vmem((2, 2, CB, HB), BF16)] * 4
        + [vmem((2, CB, HB), BF16)] * 2
        + [pltpu.SemaphoreType.DMA((N_SEND,)), pltpu.SemaphoreType.DMA((N_RECV,))]
    )
    block = pl.BlockSpec(memory_space=pltpu.VMEM)
    outs = pl.pallas_call(
        functools.partial(kernel, n0),
        out_shape=(
            jax.ShapeDtypeStruct(strip, BF16),
            jax.ShapeDtypeStruct(strip, BF16),
            jax.ShapeDtypeStruct(proj_in.shape, BF16),
            jax.ShapeDtypeStruct(proj_out.shape, BF16),
        ),
        in_specs=[block] * 7,
        out_specs=(block,) * 4,
        scratch_shapes=scratch,
        compiler_params=pltpu.CompilerParams(
            collective_id=0, has_side_effects=True, vmem_limit_bytes=56 << 20
        ),
    )(
        images,
        dw_kernel,
        norm_gain.reshape(1, CB),
        proj_in,
        proj_out,
        layer_scale.reshape(1, CB),
        cotangent.reshape(PIX, CB),
    )
    return pl.pallas_call(
        hand_out,
        out_shape=tuple(jax.ShapeDtypeStruct(out.shape, out.dtype) for out in outs),
        in_specs=[block] * 4,
        out_specs=(block,) * 4,
    )(*outs)


def solution(mesh):
    placed = (
        P(None, "row", None, "col"),
        P(None, None, "col"),
        P("col"),
        P("row", "col"),
        P("row", "col"),
        P("col"),
        P(None, "row", None, "col"),
    )
    return jax.shard_map(
        on_device,
        mesh=mesh,
        in_specs=placed,
        out_specs=(
            P(None, "row", None, "col"),
            P(None, "row", None, "col"),
            P("row", "col"),
            P("row", "col"),
        ),
        check_vma=False,
    )
```
